256 devices in a mesh: ctx: 32 (over z, x_lo, core), grp: 8 (over y, x_hi).
Axes of the slice: x: 4 (x_hi: 2, x_lo: 2; x = x_hi * 2 + x_lo), y: 4, z: 8, core: 2. Of those that a mesh axis runs over, the one named last changes fastest.
Arguments:
- prompt_x: bfloat16 [2, 16384, 8192], P(None, 'ctx', 'grp'), may hold values from -6 to 6
- prompt_b: bfloat16 [2, 16384, 2048], P(None, 'ctx', 'grp'), may hold values from -6 to 6
- prompt_c: bfloat16 [2, 16384, 2048], P(None, 'ctx', 'grp'), may hold values from -0.375 to 0.375
- prompt_step: float32 [2, 128, 16384], P(None, 'grp', 'ctx'), may hold values from 0.005 to 0.05
- prompt_decay: float32 [2, 128, 16384], P(None, 'grp', 'ctx'), may hold values from -1 to 0
- skip_weight: float32 [128], P('grp'), may hold values from 0.5 to 1.5
- decode_x: bfloat16 [4, 32, 128, 64], P(None, None, 'grp', 'ctx'), may hold values from -6 to 6
- decode_b: bfloat16 [4, 32, 2048], P(None, None, 'grp'), may hold values from -6 to 6
- decode_c: bfloat16 [4, 32, 2048], P(None, None, 'grp'), may hold values from -0.375 to 0.375
- decode_step: float32 [4, 32, 128], P(None, None, 'grp'), may hold values from 0.05 to 0.5
- decode_decay: float32 [4, 32, 128], P(None, None, 'grp'), may hold values from -0.5 to -0.01
- out_proj: bfloat16 [128, 64, 8192], P('grp', 'ctx'), may hold values from -0.0625 to 0.0625
- norm_gain: float32 [8192], replicated, may hold values from 0.5 to 1.5
- lm_head: bfloat16 [8192, 65536], P(None, ('ctx', 'grp')), may hold values from -11.932427 to 11.932427
- mask_words: int32 [16, 2048], P(None, ('ctx', 'grp')), may hold values from -2147483648 to 2147483646, as said below
- state_ids: int32 [4, 32], replicated, may hold values from 0 to 15
- chosen: int32 [4, 32], replicated, may hold values from 0 to 65535, as said below
Outputs:
- prompt_y: bfloat16 [2, 16384, 8192], P(None, 'ctx', 'grp')
- decode_state: float32 [32, 128, 64, 256], P(None, 'grp', 'ctx')
- chosen_logprob: float32 [4, 32], replicated
The draws below stay inside these ranges and needn't reach their ends.
Inputs may be any that keep to these rules, and one draw needn't show every extreme that they name: `mask_words`: bit b of word w in row q says whether token 32 w + b is allowed in automaton state q. Every chosen token is allowed by the mask row of its row's automaton state at that step.
All inputs are finite; a program needn't handle non-finite values.
Results may differ from the reference program's by a relative error of at most 0.0054.
Values sent between devices are 32-bit elements; how exact they have to be, the bound alone decides.
No kernel may reach another device: no remote copies, remote signals or barrier semaphores. Data moves between devices by JAX's collectives and lax.ppermute only.
A program may use at most 128 MiB of HBM per device.

```python
import math
import jax
import jax.numpy as jnp
from jax import lax

D = 8192
P_SIZE = 64
NST = 256
VOCAB = 65536
BLOCK = 256
STEPS = 4
PROMPT_COUNT = 2
STATES = 16
TOK_DEV = 512
GROUPS = 8
HEADS = 128
PROMPT_LENGTH = 16384
ROWS = 32


def draw_prompt_decay(key, part):
    random_keys = jax.random.split(jax.random.fold_in(key, 311), 7)
    fast_share = 0.5
    fast = jax.random.uniform(random_keys[0], (HEADS,)) < fast_share
    fast_rate = jnp.exp(jax.random.uniform(random_keys[1], (HEADS,), minval=math.log(1.0 / 50.0), maxval=math.log(1.0 / 30.0)))
    slow_rate = jnp.exp(jax.random.uniform(random_keys[2], (HEADS,), minval=math.log(0.05), maxval=math.log(0.6))) / PROMPT_LENGTH
    base_rate = jnp.where(fast, fast_rate, slow_rate)
    shard_count = PROMPT_LENGTH // TOK_DEV
    shard_factor = jnp.exp(jax.random.uniform(random_keys[3], (PROMPT_COUNT, HEADS, shard_count), minval=math.log(0.5), maxval=math.log(2.0)))
    shard_factor = jnp.repeat(shard_factor, TOK_DEV, axis=2)
    roughness = jax.random.uniform(random_keys[4], (PROMPT_COUNT, HEADS, PROMPT_LENGTH), minval=0.5, maxval=1.5)
    decay_rates = base_rate[None, :, None] * shard_factor * roughness
    spike_position = jax.random.randint(random_keys[5], (PROMPT_COUNT, 3), 0, PROMPT_LENGTH, dtype=jnp.int32)
    spike_amount = jax.random.uniform(random_keys[6], (PROMPT_COUNT, 3), minval=0.22, maxval=0.5)
    token_positions = jnp.arange(PROMPT_LENGTH, dtype=jnp.int32)
    spike_events = jnp.sum(jnp.where(token_positions[None, None, :] == spike_position[:, :, None], spike_amount[:, :, None], 0.0), axis=1)
    return -(decay_rates + spike_events[:, None, :])


def draw_lm_head(key, part):
    random_keys = jax.random.split(jax.random.fold_in(key, 523), 1)
    base = jnp.clip(jax.random.normal(random_keys[0], (D, VOCAB)), -6.0, 6.0) * (3.0 / math.sqrt(D))
    return base.astype(jnp.bfloat16)


def schema_tables(key):
    random_keys = jax.random.split(jax.random.fold_in(key, 907), 3)
    mask_table = jax.random.randint(random_keys[0], (STATES, VOCAB // 32), -2147483648, 2147483647, dtype=jnp.int32)
    state_table = jax.random.randint(random_keys[1], (STEPS, ROWS), 0, STATES, dtype=jnp.int32)
    mask_bits = (jnp.right_shift(mask_table[:, :, None], jnp.arange(32, dtype=jnp.int32)[None, None, :]) & 1).reshape(STATES, VOCAB)
    live_bits = mask_bits[state_table]
    rank_scores = jax.random.randint(random_keys[2], (STEPS, ROWS, VOCAB), 0, 16384, dtype=jnp.int32) * VOCAB + jnp.arange(VOCAB, dtype=jnp.int32)[None, None, :]
    picked = jnp.argmax(jnp.where(live_bits == 1, rank_scores, -1), axis=-1).astype(jnp.int32)
    return (mask_table, state_table, picked)


def draw_mask_words(key, part):
    return schema_tables(key)[0]


def draw_state_ids(key, part):
    return schema_tables(key)[1]


def draw_chosen(key, part):
    return schema_tables(key)[2]


def steps_of(key, dims, cuts, smallest, high):
    level, own = 1.0, jax.random.fold_in(key, 6)
    for dim, shards_of in cuts:
        heights = jnp.exp(jax.random.uniform(jax.random.fold_in(own, dim), (shards_of,), jnp.float32, smallest / len(cuts), high / len(cuts)))
        level = level * jnp.repeat(heights, dims[dim] // shards_of).reshape([-1 if axis == dim else 1 for axis in range(len(dims))])
    return level


def gaussian(rng, dims, width, reach, cuts=(), kind=jnp.bfloat16):
    level = steps_of(rng, dims, cuts, -0.22, 0.18) if cuts else 1.0
    values = jax.random.normal(rng, dims, jnp.float32) * width * level
    return jnp.minimum(jnp.maximum(values, -reach), reach).astype(kind)


def setup_inputs(seed: int = 0) -> dict:
    seeds = jax.random.split(jax.random.key(seed), 18)
    prompt_x = gaussian(seeds[0], (PROMPT_COUNT, PROMPT_LENGTH, HEADS * P_SIZE), 1.0, 6.0, ((1, 32), (2, 8)))
    prompt_b = gaussian(seeds[1], (PROMPT_COUNT, PROMPT_LENGTH, GROUPS * NST), 1.0, 6.0, ((1, 32), (2, 8)))
    prompt_c = gaussian(seeds[2], (PROMPT_COUNT, PROMPT_LENGTH, GROUPS * NST), NST ** -0.5, 0.375, ((1, 32), (2, 8)))
    prompt_step = jnp.clip(jnp.exp(math.log(0.05) - 2.3025851 * jax.random.uniform(seeds[3], (PROMPT_COUNT, HEADS, PROMPT_LENGTH), jnp.float32) ** steps_of(seeds[3], (PROMPT_COUNT, HEADS, PROMPT_LENGTH), ((1, 8), (2, 32)), -0.2, 0.2)), 0.005, 0.05)
    prompt_decay = draw_prompt_decay(jax.random.fold_in(seeds[17], 71), 0)
    skip_weight = jnp.clip(0.5 + 1.0 * jax.random.uniform(seeds[5], (HEADS,), jnp.float32) ** steps_of(seeds[5], (HEADS,), ((0, 8),), -0.2, 0.2), 0.5, 1.5)
    decode_x = gaussian(seeds[6], (STEPS, ROWS, HEADS, P_SIZE), 1.0, 6.0, ((2, 8), (3, 32)))
    decode_b = gaussian(seeds[7], (STEPS, ROWS, GROUPS * NST), 1.0, 6.0, ((2, 8),))
    decode_c = gaussian(seeds[8], (STEPS, ROWS, GROUPS * NST), NST ** -0.5, 0.375, ((2, 8),))
    decode_step = jnp.clip(jnp.exp(math.log(0.5) - 2.3025851 * jax.random.uniform(seeds[9], (STEPS, ROWS, HEADS), jnp.float32) ** steps_of(seeds[9], (STEPS, ROWS, HEADS), ((2, 8),), -0.2, 0.2)), 0.05, 0.5)
    decode_decay = jnp.clip(-0.5 + 0.49 * jax.random.uniform(seeds[10], (STEPS, ROWS, HEADS), jnp.float32) ** steps_of(seeds[10], (STEPS, ROWS, HEADS), ((2, 8),), -0.2, 0.2), -0.5, -0.01)
    out_proj = gaussian(seeds[11], (HEADS, P_SIZE, D), (HEADS * P_SIZE) ** -0.5, 0.0625, ((0, 8), (1, 32)))
    norm_gain = jnp.clip(1.0 + 0.1 * jax.random.normal(seeds[12], (D,), jnp.float32), 0.5, 1.5)
    lm_head = draw_lm_head(jax.random.fold_in(seeds[17], 71), 0)
    mask_words = draw_mask_words(jax.random.fold_in(seeds[17], 71), 0)
    state_ids = draw_state_ids(jax.random.fold_in(seeds[17], 71), 0)
    chosen = draw_chosen(jax.random.fold_in(seeds[17], 71), 0)
    return {"prompt_x": prompt_x, "prompt_b": prompt_b, "prompt_c": prompt_c, "prompt_step": prompt_step, "prompt_decay": prompt_decay, "skip_weight": skip_weight, "decode_x": decode_x, "decode_b": decode_b, "decode_c": decode_c, "decode_step": decode_step, "decode_decay": decode_decay, "out_proj": out_proj, "norm_gain": norm_gain, "lm_head": lm_head, "mask_words": mask_words, "state_ids": state_ids, "chosen": chosen}


NEG_BIG = -1e+30
EPS = 1e-05

def reference(prompt_x, prompt_b, prompt_c, prompt_step, prompt_decay, skip_weight, decode_x, decode_b, decode_c, decode_step, decode_decay, out_proj, norm_gain, lm_head, mask_words, state_ids, chosen):
    seq_count, length_all, feature_width = prompt_x.shape
    head_count = prompt_step.shape[1]
    head_dim = feature_width // head_count
    group_count = prompt_b.shape[2] // NST
    per_group = head_count // group_count
    block_count = length_all // BLOCK
    x_blocks = jnp.moveaxis(prompt_x.reshape(seq_count, block_count, BLOCK, head_count, head_dim), 1, 0)
    b_blocks = jnp.moveaxis(prompt_b.reshape(seq_count, block_count, BLOCK, group_count, NST), 1, 0)
    c_blocks = jnp.moveaxis(prompt_c.reshape(seq_count, block_count, BLOCK, group_count, NST), 1, 0)
    step_blocks = jnp.moveaxis(prompt_step.reshape(seq_count, head_count, block_count, BLOCK), 2, 0)
    decay_blocks = jnp.moveaxis(prompt_decay.reshape(seq_count, head_count, block_count, BLOCK), 2, 0)
    row_pos = lax.broadcasted_iota(jnp.int32, (BLOCK, BLOCK), 0)
    col_pos = lax.broadcasted_iota(jnp.int32, (BLOCK, BLOCK), 1)

    def one_block(entering, pieces):
        x_blk, b_blk, c_blk, step_blk, decay_blk = pieces
        running = jnp.cumsum(decay_blk, axis=2)
        block_total = running[:, :, BLOCK - 1]
        log_gap = jnp.where(col_pos <= row_pos, running[:, :, :, None] - running[:, :, None, :], -jnp.inf)
        scores = jnp.einsum('sqgn,skgn->sgqk', c_blk.astype(jnp.float32), b_blk.astype(jnp.float32), precision=lax.Precision.HIGHEST)
        scores = jnp.repeat(scores, per_group, axis=1)
        mix_weights = lax.optimization_barrier((scores * jnp.exp(log_gap) * step_blk[:, :, None, :]).astype(jnp.bfloat16))
        y_inner = jnp.einsum('shqk,skhp->sqhp', mix_weights.astype(jnp.float32), x_blk.astype(jnp.float32), precision=lax.Precision.HIGHEST)
        to_end = jnp.transpose(step_blk * jnp.exp(block_total[:, :, None] - running), (0, 2, 1))
        scaled_x = lax.optimization_barrier((x_blk * to_end[:, :, :, None]).astype(jnp.bfloat16))
        b_heads = jnp.repeat(b_blk, per_group, axis=2)
        c_heads = jnp.repeat(c_blk, per_group, axis=2)
        end_states = jnp.einsum('sqhp,sqhn->shpn', scaled_x.astype(jnp.float32), b_heads.astype(jnp.float32), precision=lax.Precision.HIGHEST)
        entering_low = lax.optimization_barrier(entering.astype(jnp.bfloat16))
        y_carry = jnp.einsum('sqhn,shpn->sqhp', c_heads.astype(jnp.float32), entering_low.astype(jnp.float32), precision=lax.Precision.HIGHEST)
        growth = jnp.transpose(jnp.exp(running), (0, 2, 1))[:, :, :, None]
        y_block = y_inner + growth * y_carry + skip_weight[None, None, :, None] * x_blk.astype(jnp.float32)
        leaving = jnp.exp(block_total)[:, :, None, None] * entering + end_states
        return (leaving, y_block.astype(jnp.bfloat16))
    start = jnp.zeros((seq_count, head_count, head_dim, NST), jnp.float32)
    final_state, y_all = lax.scan(one_block, start, (x_blocks, b_blocks, c_blocks, step_blocks, decay_blocks))
    prompt_y = jnp.moveaxis(y_all, 0, 1).reshape(seq_count, length_all, feature_width)
    row_count = decode_x.shape[1]
    state_rows = jnp.repeat(final_state, row_count // seq_count, axis=0)
    mask_bits = (jnp.right_shift(mask_words[:, :, None], jnp.arange(32, dtype=jnp.int32)[None, None, :]) & 1).reshape(mask_words.shape[0], -1)
    results = []
    for step_index in range(STEPS):
        b_heads = jnp.repeat(decode_b[step_index].reshape(row_count, group_count, NST), per_group, axis=1)
        c_heads = jnp.repeat(decode_c[step_index].reshape(row_count, group_count, NST), per_group, axis=1)
        inject = (decode_step[step_index][:, :, None] * decode_x[step_index])[:, :, :, None] * b_heads[:, :, None, :]
        state_rows = jnp.exp(decode_decay[step_index])[:, :, None, None] * state_rows + inject
        step_y = jnp.einsum('rhpn,rhn->rhp', state_rows, c_heads.astype(jnp.float32), precision=lax.Precision.HIGHEST)
        step_y = (step_y + skip_weight[None, :, None] * decode_x[step_index]).astype(jnp.bfloat16)
        layer_out = jnp.dot(step_y.reshape(row_count, head_count * head_dim), out_proj.reshape(head_count * head_dim, out_proj.shape[2]), preferred_element_type=jnp.float32)
        normed = (layer_out * lax.rsqrt(lax.optimization_barrier(jnp.mean(layer_out * layer_out, axis=1, keepdims=True)) + EPS) * norm_gain).astype(jnp.bfloat16)
        logits = jnp.dot(normed, lm_head, preferred_element_type=jnp.float32)
        allowed = mask_bits[state_ids[step_index]] == 1
        row_max = lax.optimization_barrier(jnp.max(jnp.where(allowed, logits, NEG_BIG), axis=1))
        row_total = lax.optimization_barrier(jnp.sum(jnp.where(allowed, jnp.exp(logits - row_max[:, None]), 0.0), axis=1))
        picked = jnp.take_along_axis(logits, chosen[step_index][:, None], axis=1)[:, 0]
        results.append(picked - row_max - jnp.log(row_total))
    return (prompt_y, state_rows, jnp.stack(results))
```

```python
import jax
import jax.numpy as jnp
import numpy as np
from jax import lax
from jax.experimental import pallas as pl
from jax.experimental.pallas import tpu as pltpu
from jax.sharding import Mesh
from jax.sharding import PartitionSpec as P

BLOCK = 256
STEPS = 4
Z, XL, CO, Y, XH = "z", "xl", "co", "y", "xh"
CTX = (Z, XL, CO)
GRP = (Y, XH)
ALL = (Z, XL, CO, Y, XH)
ZX = (Z, XL)
CG = (CO, Y, XH)

NEG_BIG = -1e30
EPS = 1e-05
F32 = jnp.float32
BF16 = jnp.bfloat16
HI = lax.Precision.HIGHEST


def size_of(axes):
    return int(np.prod([lax.axis_size(a) for a in axes]))


def iota(shape, dim):
    return lax.broadcasted_iota(jnp.int32, shape, dim)


def dot(a, b, dims, precision=None):
    return lax.dot_general(a, b, (dims, ((), ())), precision=precision, preferred_element_type=F32)


def swapped(value):
    return lax.ppermute(value, CO, [(0, 1), (1, 0)])


def told(value, axes):
    many = size_of(axes)
    return lax.all_to_all(
        jnp.broadcast_to(value[None], (many, *value.shape)), axes, 0, 0, tiled=True
    )


def column(row, rows, per):
    width = row.shape[1]
    pick = iota((rows, width), 1) == iota((rows, width), 0) // per
    return jnp.sum(jnp.where(pick, row, 0.0), axis=1, keepdims=True)


def local_index(feature, my_core, head_dim, zx, p2, heads):
    h, p = feature // head_dim, feature % head_dim
    chip, rest = p // (2 * p2), p % (2 * p2)
    side = (rest // p2) ^ my_core
    return ((side * zx + chip) * heads + h) * p2 + rest % p2


def states_kernel(zx, p2, core, x, b, step, decay, e0, keep, send, run_out, logs):
    tokens, width = x.shape[1], x.shape[2]
    heads = step.shape[1]
    head_dim = width // heads
    half = width // 2
    blocks = tokens // BLOCK
    upper = (iota((BLOCK, BLOCK), 0) <= iota((BLOCK, BLOCK), 1)).astype(F32)
    expand = (iota((heads, width), 1) // head_dim == iota((heads, width), 0)).astype(F32)
    goes = local_index(iota((1, width), 1), core[0], head_dim, zx, p2, heads)
    perm_t = (iota((width, width), 0) == goes).astype(BF16)
    of_row = (iota((width, heads), 0) // p2 % heads == iota((width, heads), 1)).astype(F32)
    lane = iota((heads, BLOCK), 1) == iota((heads, BLOCK), 0)
    state = None
    total_row = jnp.zeros((1, BLOCK), F32)
    for k in range(blocks):
        at = slice(k * BLOCK, (k + 1) * BLOCK)
        run = dot(decay[0, :, at], upper, ((1,), (0,)), HI)
        run_out[0, :, at] = run
        total = jnp.broadcast_to(run[:, BLOCK - 1 :], (heads, BLOCK))
        to_end = step[0, :, at] * jnp.exp(total - run)
        spread = dot(to_end.T, expand, ((1,), (0,)), HI)
        scaled = (x[0, at].astype(F32) * spread).astype(BF16)
        moved = dot(perm_t, scaled, ((1,), (1,))).astype(BF16)
        own = dot(moved, b[0, at], ((1,), (0,)))
        total_row = total_row + jnp.sum(jnp.where(lane, total, 0.0), axis=0, keepdims=True)
        if k == 0:
            state = own
            e0[0] = own
            logs[0] = jnp.broadcast_to(total_row, (8, BLOCK))
        else:
            state = dot(of_row, jnp.exp(total), ((1,), (0,)), HI) * state + own
    keep[0] = state[:half]
    send[0, :half] = state[half:]
    send[0, half:] = jnp.broadcast_to(total_row, (8, BLOCK))


def pair_kernel(zx, p2, heads, core, keep, own_log, came, out):
    rows = heads * p2
    first = core[0] == 0
    half = zx * rows
    for s in range(keep.shape[0]):
        mine = own_log[s, :1]
        other = came[s, half : half + 1]
        f_mine = jnp.where(first, jnp.exp(column(other, rows, p2)), 1.0)
        f_came = jnp.where(first, 1.0, jnp.exp(column(mine, rows, p2)))
        for k in range(zx):
            at = slice(k * rows, (k + 1) * rows)
            out[k, s * rows : (s + 1) * rows] = f_mine * keep[s, at] + f_came * came[s, at]
            out[k, 2 * rows + s * 4 : 2 * rows + s * 4 + 4] = jnp.broadcast_to(
                mine + other, (4, mine.shape[1])
            )


def scan_kernel(
    p2, heads, pieces, c_q, b_q, cum, x_q, step_q, skip_col, enter, step_y, row_state
):
    zx = pieces.shape[0]
    rows = heads * p2
    many = x_q.shape[1]
    half = many // 2
    per = half // STEPS
    final = jnp.zeros((2 * rows, pieces.shape[2]), F32)
    for k in range(zx):
        enter[k] = final
        fac = jnp.concatenate(
            [
                jnp.exp(column(pieces[k, 2 * rows + 4 * s : 2 * rows + 4 * s + 1], rows, p2))
                for s in range(2)
            ],
            axis=0,
        )
        final = fac * final + pieces[k, : 2 * rows]
    cums = cum[...]
    grow = jnp.exp(cums)
    xs = x_q[...] * step_q[...] * jnp.exp(-cums)
    c_all = c_q[...].astype(F32)
    b_all = b_q[...].astype(F32)
    from_state = [
        dot(final[s * rows : (s + 1) * rows], c_all, ((1,), (1,)), HI) for s in range(2)
    ]
    lane = iota((rows, many), 1)
    seen = jnp.where(lane < half, from_state[0], from_state[1])
    cross = dot(b_all, c_all, ((1,), (1,)), HI)
    earlier, later = iota((many, many), 0), iota((many, many), 1)
    same = (earlier // half == later // half) & (earlier % per == later % per)
    cross = jnp.where(same & (earlier <= later), cross, 0.0)
    seen = seen + dot(xs, cross, ((1,), (0,)), HI)
    y = grow * seen + skip_col[...] * x_q[...]
    step_y[...] = y.astype(BF16).astype(F32)
    for s in range(2):
        for r in range(per):
            value = final[s * rows : (s + 1) * rows]
            for i in range(STEPS):
                q = s * half + i * per + r
                value = value + xs[:, q : q + 1] * b_all[q : q + 1]
            row_state[s * per + r] = grow[:, q : q + 1] * value


def project_kernel(y, w, out):
    groups, rows, many = y.shape
    left = y[...].reshape(groups * rows, many).T.astype(BF16)
    right = w[...].reshape(groups * rows, w.shape[2]).astype(BF16)
    out[...] = dot(left, right, ((1,), (0,)))


def logits_kernel(core, own, other, gain, head, allowed, chosen, out):
    blocks, many, width = own.shape
    half = blocks * width
    total = jnp.zeros((many, 1), F32)
    for ref in (own, other):
        for k in range(blocks):
            part = ref[k]
            total = total + jnp.sum(part * part, axis=1, keepdims=True)
    scale = lax.rsqrt(total / (2 * half) + EPS)
    acc = jnp.zeros((head.shape[1], many), F32)
    for side, ref in enumerate((own, other)):
        start = (core[0] ^ side) * half
        for k in range(blocks):
            at = pl.ds(pl.multiple_of(start + k * width, width), width)
            normed = (ref[k] * scale * gain[:, at]).astype(BF16)
            acc = acc + dot(head[at], normed, ((0,), (1,)))
    ok = allowed[...] > 0.5
    top = jnp.max(jnp.where(ok, acc, NEG_BIG), axis=0, keepdims=True)
    total = jnp.sum(jnp.where(ok, jnp.exp(acc - top), 0.0), axis=0, keepdims=True)
    hit = iota(acc.shape, 0) == chosen[...]
    picked = jnp.sum(jnp.where(hit, acc, 0.0), axis=0, keepdims=True)
    out[0:1] = top
    out[1:2] = total
    out[2:3] = picked
    out[3:8] = jnp.zeros((5, many), F32)


def outputs_kernel(zx, p2, core, x, b, c, step, run, logs, own, other, e0, skip, out):
    width = x.shape[2]
    heads = step.shape[1]
    head_dim = width // heads
    rows = heads * p2
    k = pl.program_id(1)
    xb, cb = x[0], c[0]
    running, steps = run[0], step[0]
    run_t = running.T
    causal = iota((BLOCK, BLOCK), 1) <= iota((BLOCK, BLOCK), 0)
    scores = jnp.where(causal, dot(cb, b[0], ((1,), (1,))), 0.0)
    enter = jnp.concatenate(
        [own[:, 0].reshape(zx * rows, -1), other[:, 0].reshape(zx * rows, -1)], axis=0
    )
    fade = jnp.where(k == 0, 1.0, jnp.exp(column(logs[0, :1], rows, p2)))
    later = jnp.where(k == 0, 0.0, 1.0)
    n = enter.shape[1]
    enter = (enter.reshape(2 * zx, rows, n) * fade[None]).reshape(width, n) + later * e0[0]
    goes = local_index(iota((width, 1), 0), core[0], head_dim, zx, p2, heads)
    perm = (iota((width, width), 1) == goes).astype(BF16)
    enter = dot(perm, enter.astype(BF16), ((1,), (0,))).astype(BF16)
    carry = dot(cb, enter, ((1,), (1,)))
    expand = (iota((heads, width), 1) // head_dim == iota((heads, width), 0)).astype(F32)
    growth = dot(jnp.exp(run_t), expand, ((1,), (0,)), HI)
    base = growth * carry + skip[...] * xb.astype(F32)
    pair = 2 * head_dim
    left = iota((BLOCK, pair), 1) < head_dim
    for j in range(heads // 2):
        at = slice(j * pair, (j + 1) * pair)
        halves = []
        for h in (2 * j, 2 * j + 1):
            gap = jnp.minimum(run_t[:, h : h + 1] - running[h : h + 1], 0.0)
            mix = (scores * jnp.exp(gap) * steps[h : h + 1]).astype(BF16)
            halves.append(dot(mix, xb[:, at], ((1,), (0,))))
        inner = jnp.where(left, halves[0], halves[1])
        out[0, :, at] = (inner + base[:, at]).astype(BF16)


def merge(parts):
    top = jnp.max(parts[:, 0], axis=0)
    total = jnp.sum(parts[:, 1] * jnp.exp(parts[:, 0] - top), axis=0)
    picked = jnp.sum(parts[:, 2], axis=0)
    return top, total, picked


def full(shape):
    return pl.BlockSpec(shape, lambda *_: (0,) * len(shape))


def call(kernel, outs, name, *args, smem=(), limit=None):
    specs = [
        pl.BlockSpec(memory_space=pltpu.SMEM) if k in smem else full(a.shape)
        for k, a in enumerate(args)
    ]
    many = isinstance(outs, tuple)
    return pl.pallas_call(
        kernel,
        grid=(1,),
        in_specs=specs,
        out_specs=tuple(full(o.shape) for o in outs) if many else full(outs.shape),
        out_shape=outs,
        name=name,
    )(*args)


def shaped(*shape, dtype=F32):
    return jax.ShapeDtypeStruct(shape, dtype)


def body(
    prompt_x,
    prompt_b,
    prompt_c,
    prompt_step,
    prompt_decay,
    skip_weight,
    decode_x,
    decode_b,
    decode_c,
    decode_step,
    decode_decay,
    out_proj,
    norm_gain,
    lm_head,
    mask_words,
    state_ids,
    chosen,
):
    seqs, tokens, width = prompt_x.shape
    n = prompt_b.shape[2]
    heads = prompt_step.shape[1]
    zx, cg, grp = size_of(ZX), size_of(CG), size_of(GRP)
    p2 = decode_x.shape[3]
    rows = heads * p2
    half = width // 2
    blocks = tokens // BLOCK
    decode_rows = decode_x.shape[1]
    per = decode_rows // seqs
    many = STEPS * decode_rows
    core = lax.axis_index(CO).astype(jnp.int32)[None]

    model = out_proj.shape[2]
    wide = model // cg
    w_rows = out_proj.astype(F32).reshape(rows, cg, wide).transpose(1, 0, 2)
    w_own = lax.all_to_all(w_rows, CG, 0, 0, tiled=True)

    def by_q(value):
        shape = value.shape[2:]
        value = value.reshape(STEPS, seqs, per, *shape)
        return jnp.moveaxis(value, 1, 0).reshape(many, *shape)

    c_q, b_q = by_q(decode_c), by_q(decode_b)
    cum_q = jnp.repeat(by_q(jnp.cumsum(decode_decay, axis=0)).T, p2, axis=0)
    step_q = jnp.repeat(by_q(decode_step).T, p2, axis=0)
    x_q = by_q(decode_x.astype(F32).reshape(STEPS, decode_rows, rows)).T
    skip_col = jnp.repeat(skip_weight, p2)[:, None]
    vocab = lm_head.shape[1]
    first = (lax.axis_index(CTX) * size_of(GRP) + lax.axis_index(GRP)) * vocab
    chosen_q = (by_q(chosen) - first)[None]
    ids_q = by_q(state_ids)
    bits = (
        jnp.right_shift(mask_words[:, :, None], jnp.arange(32, dtype=jnp.int32)[None, None]) & 1
    ).reshape(mask_words.shape[0], vocab)
    onehot = (ids_q[None] == jnp.arange(mask_words.shape[0])[:, None]).astype(BF16)
    allowed = dot(bits.astype(BF16), onehot, ((0,), (0,)))

    by_s = lambda *shape: pl.BlockSpec((1, *shape), lambda s: (s,) + (0,) * len(shape))
    e0, keep, send, run, logs = pl.pallas_call(
        lambda *refs: states_kernel(zx, p2, *refs),
        grid=(seqs,),
        in_specs=[
            pl.BlockSpec(memory_space=pltpu.SMEM),
            by_s(tokens, width),
            by_s(tokens, n),
            by_s(heads, tokens),
            by_s(heads, tokens),
        ],
        out_specs=(
            by_s(width, n),
            by_s(half, n),
            by_s(half + 8, n),
            by_s(heads, tokens),
            by_s(8, n),
        ),
        out_shape=(
            shaped(seqs, width, n),
            shaped(seqs, half, n),
            shaped(seqs, half + 8, n),
            shaped(seqs, heads, tokens),
            shaped(seqs, 8, n),
        ),
        name="states",
    )(core, prompt_x, prompt_b, prompt_step, prompt_decay)
    came = swapped(send)
    own_log = send[:, half:]
    pieces = call(
        lambda *refs: pair_kernel(zx, p2, heads, *refs),
        shaped(zx, 2 * rows + 8, n),
        "pair",
        core,
        keep,
        own_log,
        came,
        smem=(0,),
    )
    pieces = lax.all_to_all(pieces, ZX, 0, 0, tiled=True)
    enter, step_y, row_state = call(
        lambda *refs: scan_kernel(p2, heads, *refs),
        (shaped(zx, 2 * rows, n), shaped(rows, many), shaped(decode_rows, rows, n)),
        "scan",
        pieces,
        c_q,
        b_q,
        cum_q,
        x_q,
        step_q,
        skip_col,
    )
    decode_state = row_state.reshape(decode_rows, heads, p2, n)

    ys = told(step_y, CG)
    partial = call(project_kernel, shaped(many, wide), "project", ys, w_own)
    partial = lax.all_to_all(partial.reshape(zx, many // zx, wide), ZX, 0, 0, tiled=True)
    summed = jnp.sum(partial, axis=0)
    own_cols = told(summed, ZX).reshape(many, wide)
    own_half = told(own_cols, GRP)
    other_half = swapped(own_half)

    parts = call(
        logits_kernel,
        shaped(8, many),
        "logits",
        core,
        own_half,
        other_half,
        norm_gain[None],
        lm_head,
        allowed,
        chosen_q,
        smem=(0,),
    )
    parts = jnp.stack(merge(told(parts[:3], (Z, CO))))
    top, total, picked = merge(told(parts, (XL, Y, XH)))
    logprob = picked - top - jnp.log(total)
    logprob = logprob.reshape(seqs, STEPS, per).transpose(1, 0, 2).reshape(STEPS, decode_rows)

    back = lax.all_to_all(enter, ZX, 0, 0, tiled=True).reshape(zx, seqs, rows, n)
    is_first = core[0] == 0

    def after(log_row, value, state):
        fade = jnp.exp(jnp.repeat(log_row[:, 0, :heads], p2, axis=1))[None, :, :, None]
        state = state[:, :half].reshape(seqs, zx, rows, n).transpose(1, 0, 2, 3)
        return fade * value + state

    for_me = jnp.where(is_first, back, after(came[:, half:], back, came))
    for_other = jnp.where(is_first, after(own_log, back, keep), back)
    other_side = swapped(for_other)

    at_k = lambda *shape: pl.BlockSpec((1, BLOCK, *shape), lambda s, k: (s, k, 0))
    lanes_k = pl.BlockSpec((1, heads, BLOCK), lambda s, k: (s, 0, k))
    states_s = pl.BlockSpec((zx, 1, rows, n), lambda s, k: (0, s, 0, 0))
    prompt_y = pl.pallas_call(
        lambda *refs: outputs_kernel(zx, p2, *refs),
        grid=(seqs, blocks),
        in_specs=[
            pl.BlockSpec(memory_space=pltpu.SMEM),
            at_k(width),
            at_k(n),
            at_k(n),
            lanes_k,
            lanes_k,
            pl.BlockSpec((1, 8, n), lambda s, k: (s, 0, 0)),
            states_s,
            states_s,
            pl.BlockSpec((1, width, n), lambda s, k: (s, 0, 0)),
            full((1, width)),
        ],
        out_specs=at_k(width),
        out_shape=shaped(seqs, tokens, width, dtype=BF16),
        name="outputs",
    )(
        core,
        prompt_x,
        prompt_b,
        prompt_c,
        prompt_step,
        run,
        logs,
        for_me,
        other_side,
        e0,
        jnp.repeat(skip_weight, width // heads)[None],
    )
    return (prompt_y, decode_state, logprob)


def solution(mesh):
    ctx, grp = mesh.devices.shape
    shape = (ctx // 4, 2, 2, grp // 2, 2)
    finer = Mesh(mesh.devices.reshape(shape), ALL)
    in_specs = (
        P(None, CTX, GRP),
        P(None, CTX, GRP),
        P(None, CTX, GRP),
        P(None, GRP, CTX),
        P(None, GRP, CTX),
        P(GRP),
        P(None, None, GRP, CTX),
        P(None, None, GRP),
        P(None, None, GRP),
        P(None, None, GRP),
        P(None, None, GRP),
        P(GRP, CTX, None),
        P(),
        P(None, ALL),
        P(None, ALL),
        P(),
        P(),
    )
    out_specs = (P(None, CTX, GRP), P(None, GRP, CTX, None), P())
    return jax.shard_map(body, mesh=finer, in_specs=in_specs, out_specs=out_specs, check_vma=False)
```

```python
import jax
import jax.numpy as jnp
import numpy as np
from jax import lax
from jax.experimental import pallas as pl
from jax.experimental.pallas import tpu as pltpu
from jax.sharding import Mesh
from jax.sharding import PartitionSpec as P


BLOCK = 256
STEPS = 4
Z, XL, CO, Y, XH = "z", "xl", "co", "y", "xh"
CTX = (Z, XL, CO)
GRP = (Y, XH)
ALL = (Z, XL, CO, Y, XH)
ZX = (Z, XL)
CG = (CO, Y, XH)

NEG_BIG = -1e30
EPS = 1e-05
F32 = jnp.float32
BF16 = jnp.bfloat16
HI = lax.Precision.HIGHEST


def size_of(axes):
    return int(np.prod([lax.axis_size(a) for a in axes]))


def iota(shape, dim):
    return lax.broadcasted_iota(jnp.int32, shape, dim)


def dot(a, b, dims, precision=None):
    return lax.dot_general(a, b, (dims, ((), ())), precision=precision, preferred_element_type=F32)


def in_thirds(value, axis):
    high = value.astype(BF16)
    rest = value - high.astype(F32)
    middle = rest.astype(BF16)
    low = (rest - middle.astype(F32)).astype(BF16)
    return jnp.concatenate([high, middle, low], axis=axis)


def one_hot_thirds(shape, axis, match):
    return jnp.concatenate([match(shape).astype(BF16)] * 3, axis=axis)


def expander(heads, width):
    per = width // heads
    return one_hot_thirds(
        (heads, width), 0, lambda shape: iota(shape, 1) // per == iota(shape, 0)
    )


def swapped(value):
    return lax.ppermute(value, CO, [(0, 1), (1, 0)])


def told(value, axes):
    many = size_of(axes)
    return lax.all_to_all(
        jnp.broadcast_to(value[None], (many, *value.shape)), axes, 0, 0, tiled=True
    )


def column(row, rows, per):
    width = row.shape[1]
    pick = iota((rows, width), 1) == iota((rows, width), 0) // per
    return jnp.sum(jnp.where(pick, row, 0.0), axis=1, keepdims=True)


def local_index(feature, my_core, head_dim, zx, p2, heads):
    h, p = feature // head_dim, feature % head_dim
    chip, rest = p // (2 * p2), p % (2 * p2)
    side = (rest // p2) ^ my_core
    return ((side * zx + chip) * heads + h) * p2 + rest % p2


def states_kernel(zx, p2, core, x, b, step, decay, e0, keep, send, run_out, logs, perm_t):
    tokens, width = x.shape[1], x.shape[2]
    heads = step.shape[1]
    head_dim = width // heads
    half = width // 2
    blocks = tokens // BLOCK

    @pl.when(pl.program_id(0) == 0)
    def _():
        goes = local_index(iota((1, width), 1), core[0], head_dim, zx, p2, heads)
        perm_t[...] = (iota((width, width), 0) == goes).astype(BF16)

    upper = (iota((BLOCK, BLOCK), 0) <= iota((BLOCK, BLOCK), 1)).astype(BF16)
    of_row = one_hot_thirds(
        (width, heads), 1, lambda shape: iota(shape, 0) // p2 % heads == iota(shape, 1)
    )
    lane = iota((heads, BLOCK), 1) == iota((heads, BLOCK), 0)
    total_row = jnp.zeros((1, BLOCK), F32)
    to_end, totals = [], []
    for k in range(blocks):
        at = slice(k * BLOCK, (k + 1) * BLOCK)
        run = dot(in_thirds(decay[0, :, at], 0), upper, ((1,), (0,)))
        run = run[:heads] + run[heads : 2 * heads] + run[2 * heads :]
        run_out[0, :, at] = run
        total = jnp.broadcast_to(run[:, BLOCK - 1 :], (heads, BLOCK))
        to_end.append(step[0, :, at] * jnp.exp(total - run))
        totals.append(total)
        total_row = total_row + jnp.sum(jnp.where(lane, total, 0.0), axis=0, keepdims=True)
        if k == 0:
            logs[0, :4] = jnp.broadcast_to(total_row, (4, BLOCK))
    logs[0, 4:] = jnp.broadcast_to(total_row, (4, BLOCK))
    send[0, half:] = jnp.broadcast_to(total_row, (8, BLOCK))
    ends = in_thirds(jnp.concatenate(to_end, axis=1).T, 1)
    spread = dot(ends, expander(heads, width), ((1,), (0,)))
    scaled = (x[0].astype(F32) * spread).astype(BF16)
    moved = dot(perm_t[...], scaled, ((1,), (1,))).astype(BF16)
    state = None
    for k in range(blocks):
        at = slice(k * BLOCK, (k + 1) * BLOCK)
        own = dot(moved[:, at], b[0, at], ((1,), (0,)))
        if k == 0:
            state = own
            e0[0] = own
        else:
            fade = dot(of_row, in_thirds(jnp.exp(totals[k]), 0), ((1,), (0,)))
            state = fade * state + own
    keep[0] = state[:half]
    send[0, :half] = state[half:]


def pair_kernel(p2, heads, core, keep, logs, came, came_logs, out):
    rows = heads * p2
    first = core[0] == 0
    for s in range(keep.shape[0]):
        mine = logs[s, 4:5]
        other = came_logs[s, :1]
        f_mine = jnp.where(first, jnp.exp(column(other, rows, p2)), 1.0)
        f_came = jnp.where(first, 1.0, jnp.exp(column(mine, rows, p2)))
        for k in range(keep.shape[1] // rows):
            at = slice(k * rows, (k + 1) * rows)
            out[k, s * rows : (s + 1) * rows] = f_mine * keep[s, at] + f_came * came[s, at]
            out[k, 2 * rows + s * 4 : 2 * rows + s * 4 + 4] = jnp.broadcast_to(
                mine + other, (4, mine.shape[1])
            )


def tables_kernel(p2, heads, c_q, b_q, cum, x_q, step_q, skip_col, grow, xs, add):
    rows, many = x_q.shape
    half = many // 2
    per = half // STEPS
    repeat = (iota((rows, heads), 0) // p2 == iota((rows, heads), 1)).astype(F32)
    cums = dot(repeat, cum[...], ((1,), (0,)), HI)
    steps = dot(repeat, step_q[...], ((1,), (0,)), HI)
    growth = jnp.exp(cums)
    inject = x_q[...] * steps * jnp.exp(-cums)
    cross = dot(b_q[...], c_q[...], ((1,), (1,)))
    earlier, later = iota((many, many), 0), iota((many, many), 1)
    same = (earlier // half == later // half) & (earlier % per == later % per)
    cross = jnp.where(same & (earlier <= later), cross, 0.0)
    grow[...] = growth
    xs[...] = inject
    add[...] = growth * dot(inject, cross, ((1,), (0,)), HI) + skip_col[...] * x_q[...]


def scan_kernel(p2, heads, pieces, c_q, grow, add, enter, step_y, last):
    zx = pieces.shape[0]
    rows = heads * p2
    many = c_q.shape[0]
    final = jnp.zeros((2 * rows, pieces.shape[2]), F32)
    for k in range(zx):
        enter[k] = final
        fac = jnp.concatenate(
            [
                jnp.exp(column(pieces[k, 2 * rows + 4 * s : 2 * rows + 4 * s + 1], rows, p2))
                for s in range(2)
            ],
            axis=0,
        )
        final = fac * final + pieces[k, : 2 * rows]
    last[...] = final
    seen = dot(final, c_q[...].astype(F32), ((1,), (1,)), HI)
    lane = iota((rows, many), 1)
    seen = jnp.where(lane < many // 2, seen[:rows], seen[rows:])
    y = grow[...] * seen + add[...]
    step_y[...] = jnp.broadcast_to(y.astype(BF16).astype(F32), step_y.shape)


def rows_kernel(last, b_q, grow, xs, row_state):
    rows, many = xs.shape
    half = many // 2
    per = half // STEPS
    b_all = b_q[...].astype(F32)
    growth, inject = grow[...], xs[...]
    for s in range(2):
        for r in range(per):
            value = last[s * rows : (s + 1) * rows]
            for i in range(STEPS):
                q = s * half + i * per + r
                value = value + inject[:, q : q + 1] * b_all[q : q + 1]
            row_state[s * per + r] = growth[:, q : q + 1] * value


def project_kernel(ny, nxh, place, own, other, *refs):
    pieces, out = refs[:-1], refs[-1]
    left, right = [], []
    for number, piece in enumerate(pieces):
        dy, dx = number // nxh, number % nxh
        at = lax.rem(place[1] + (ny - dy), ny) * nxh + lax.rem(place[2] + (nxh - dx), nxh)
        left += [own[at], other[at]]
        right.append(piece[...].reshape(-1, piece.shape[2]))
    left = jnp.concatenate(left, axis=0).T.astype(BF16)
    right = jnp.concatenate(right, axis=0).astype(BF16)
    out[...] = dot(left, right, ((1,), (0,)))


def logits_kernel(ny, nxh, steps, place, *refs):
    arrays, (gain, head, allowed, chosen, out) = refs[: 2 * len(steps)], refs[2 * len(steps) :]
    many, width = arrays[0].shape
    model = head.shape[0]
    total = jnp.zeros((many, 128), F32)
    for ref in arrays:
        part = ref[...]
        part = part * part
        for k in range(width // 128):
            total = total + part[:, k * 128 : (k + 1) * 128]
    scale = lax.rsqrt(jnp.sum(total, axis=1, keepdims=True) / model + EPS)
    acc = jnp.zeros((many, head.shape[1]), F32)
    for number, ref in enumerate(arrays):
        side, (dy, dx) = number // len(steps), steps[number % len(steps)]
        of_y = lax.rem(place[1] + (ny - dy), ny)
        of_x = lax.rem(place[2] + (nxh - dx), nxh)
        block = ((place[0] ^ side) * ny + of_y) * nxh + of_x
        at = pl.ds(pl.multiple_of(block * width, width), width)
        normed = (ref[...] * scale * gain[:, at]).astype(BF16)
        acc = acc + dot(normed, head[at], ((1,), (0,)))
    acc = acc.T
    ok = allowed[...] > 0.5
    top = jnp.max(jnp.where(ok, acc, NEG_BIG), axis=0, keepdims=True)
    total = jnp.sum(jnp.where(ok, jnp.exp(acc - top), 0.0), axis=0, keepdims=True)
    hit = iota(acc.shape, 0) == chosen[...]
    picked = jnp.sum(jnp.where(hit, acc, 0.0), axis=0, keepdims=True)
    out[...] = jnp.broadcast_to(jnp.concatenate([top, total, picked], axis=0)[None], out.shape)


def inner_kernel(x, b, c, step, run, skip, out):
    width = x.shape[2]
    heads = step.shape[1]
    head_dim = width // heads
    xb = x[0]
    running, steps = run[0], step[0]
    run_t = running.T
    causal = iota((BLOCK, BLOCK), 1) <= iota((BLOCK, BLOCK), 0)
    scores = jnp.where(causal, dot(c[0], b[0], ((1,), (1,))), 0.0)
    pair = 2 * head_dim
    left = iota((BLOCK, pair), 1) < head_dim
    for j in range(heads // 2):
        at = slice(j * pair, (j + 1) * pair)
        halves = []
        for h in (2 * j, 2 * j + 1):
            gap = jnp.minimum(run_t[:, h : h + 1] - running[h : h + 1], 0.0)
            mix = (scores * jnp.exp(gap) * steps[h : h + 1]).astype(BF16)
            halves.append(dot(mix, xb[:, at], ((1,), (0,))))
        inner = jnp.where(left, halves[0], halves[1])
        out[0, :, at] = inner + skip[:, at] * xb[:, at].astype(F32)


def carry_kernel(zx, p2, heads, core, inner, c, run, logs, own, other, e0, *refs):
    out, perm = refs[-2:]
    tokens, width = inner.shape[1], inner.shape[2]
    head_dim = width // heads
    rows = heads * p2
    blocks = tokens // BLOCK
    goes = local_index(iota((width, 1), 0), core[0], head_dim, zx, p2, heads)
    perm[...] = (iota((width, width), 1) == goes).astype(BF16)
    enter = jnp.concatenate(
        [own[:, 0].reshape(zx * rows, -1), other[:, 0].reshape(zx * rows, -1)], axis=0
    )
    n = enter.shape[1]
    fade = jnp.exp(column(logs[0, :1], rows, p2))
    after = (enter.reshape(2 * zx, rows, n) * fade[None]).reshape(width, n) + e0[0]
    both = jnp.concatenate([enter.astype(BF16), after.astype(BF16)], axis=1)
    both = dot(perm[...], both, ((1,), (0,))).astype(BF16)
    growth = dot(in_thirds(jnp.exp(run[0].T), 1), expander(heads, width), ((1,), (0,)))
    for k in range(blocks):
        at = slice(k * BLOCK, (k + 1) * BLOCK)
        carry = dot(c[0, at], both[:, k * n : (k + 1) * n], ((1,), (1,)))
        out[0, at] = (inner[0, at] + growth[at] * carry).astype(BF16)


def merge(parts):
    top = jnp.max(parts[:, 0], axis=0)
    total = jnp.sum(parts[:, 1] * jnp.exp(parts[:, 0] - top), axis=0)
    picked = jnp.sum(parts[:, 2], axis=0)
    return top, total, picked


def full(shape):
    return pl.BlockSpec(shape, lambda *_: (0,) * len(shape))


def call(kernel, outs, *args, smem=(), anywhere=()):
    def spec(k, arg):
        if k in smem:
            return pl.BlockSpec(memory_space=pltpu.SMEM)
        if k in anywhere:
            return pl.BlockSpec(memory_space=pl.ANY)
        return full(arg.shape)

    specs = [spec(k, arg) for k, arg in enumerate(args)]
    many = isinstance(outs, tuple)
    return pl.pallas_call(
        kernel,
        grid=(1,),
        in_specs=specs,
        out_specs=tuple(full(o.shape) for o in outs) if many else full(outs.shape),
        out_shape=outs,
    )(*args)


def shaped(*shape, dtype=F32):
    return jax.ShapeDtypeStruct(shape, dtype)


def body(
    prompt_x,
    prompt_b,
    prompt_c,
    prompt_step,
    prompt_decay,
    skip_weight,
    decode_x,
    decode_b,
    decode_c,
    decode_step,
    decode_decay,
    out_proj,
    norm_gain,
    lm_head,
    mask_words,
    state_ids,
    chosen,
):
    seqs, tokens, width = prompt_x.shape
    n = prompt_b.shape[2]
    heads = prompt_step.shape[1]
    zx, cg, grp = size_of(ZX), size_of(CG), size_of(GRP)
    p2 = decode_x.shape[3]
    rows = heads * p2
    half = width // 2
    blocks = tokens // BLOCK
    decode_rows = decode_x.shape[1]
    per = decode_rows // seqs
    many = STEPS * decode_rows
    core = lax.axis_index(CO).astype(jnp.int32)[None]

    model = out_proj.shape[2]
    wide = model // cg
    ny, nxh = lax.axis_size(Y), lax.axis_size(XH)
    iy, ixh = (lax.axis_index(a).astype(jnp.int32) for a in (Y, XH))
    place = jnp.stack([core[0], iy, ixh])
    grp_steps = [(dy, dx) for dy in range(ny) for dx in range(nxh)]

    def grp_perm(dy, dx):
        return [
            (y * nxh + x, (y + dy) % ny * nxh + (x + dx) % nxh)
            for y in range(ny)
            for x in range(nxh)
        ]

    w_rows = out_proj.astype(F32).reshape(rows, 2, grp, wide).transpose(1, 2, 0, 3)
    w_keep = lax.dynamic_index_in_dim(w_rows, core[0], 0, keepdims=False)
    w_other = lax.dynamic_index_in_dim(w_rows, 1 - core[0], 0, keepdims=False)
    w_came = swapped(w_other)
    w_both = jnp.stack([w_keep, w_came], axis=1)
    w_own = []
    for dy, dx in grp_steps:
        to = (iy + dy) % ny * nxh + (ixh + dx) % nxh
        part = lax.dynamic_index_in_dim(w_both, to, 0, keepdims=False)
        w_own.append(lax.ppermute(part, GRP, grp_perm(dy, dx)) if dy or dx else part)

    def by_q(value):
        shape = value.shape[2:]
        value = value.reshape(STEPS, seqs, per, *shape)
        return jnp.moveaxis(value, 1, 0).reshape(many, *shape)

    c_q, b_q = by_q(decode_c), by_q(decode_b)
    cum_q = by_q(jnp.cumsum(decode_decay, axis=0)).T
    step_q = by_q(decode_step).T
    x_q = by_q(decode_x.astype(F32).reshape(STEPS, decode_rows, rows)).T
    skip_col = jnp.repeat(skip_weight, p2)[:, None]
    vocab = lm_head.shape[1]
    first = (lax.axis_index(CTX) * size_of(GRP) + lax.axis_index(GRP)) * vocab
    chosen_q = (by_q(chosen) - first)[None]
    ids_q = by_q(state_ids)
    bits = (
        jnp.right_shift(mask_words[:, :, None], jnp.arange(32, dtype=jnp.int32)[None, None]) & 1
    ).reshape(mask_words.shape[0], vocab)
    onehot = (ids_q[None] == jnp.arange(mask_words.shape[0])[:, None]).astype(BF16)
    allowed = dot(bits.astype(BF16), onehot, ((0,), (0,)))

    by_s = lambda *shape: pl.BlockSpec((1, *shape), lambda s: (s,) + (0,) * len(shape))
    e0, keep, send, run, logs = pl.pallas_call(
        lambda *refs: states_kernel(zx, p2, *refs),
        grid=(seqs,),
        in_specs=[
            pl.BlockSpec(memory_space=pltpu.SMEM),
            by_s(tokens, width),
            by_s(tokens, n),
            by_s(heads, tokens),
            by_s(heads, tokens),
        ],
        out_specs=(
            by_s(width, n),
            by_s(half, n),
            by_s(half + 8, n),
            by_s(heads, tokens),
            by_s(8, n),
        ),
        out_shape=(
            shaped(seqs, width, n),
            shaped(seqs, half, n),
            shaped(seqs, half + 8, n),
            shaped(seqs, heads, tokens),
            shaped(seqs, 8, n),
        ),
        scratch_shapes=[pltpu.VMEM((width, width), BF16)],
        name="states",
    )(core, prompt_x, prompt_b, prompt_step, prompt_decay)
    at_k = lambda *shape: pl.BlockSpec((1, BLOCK, *shape), lambda s, k: (s, k, 0))
    lanes_k = pl.BlockSpec((1, heads, BLOCK), lambda s, k: (s, 0, k))
    came = swapped(send)
    inner = pl.pallas_call(
        inner_kernel,
        grid=(seqs, blocks),
        in_specs=[at_k(width), at_k(n), at_k(n), lanes_k, lanes_k, full((1, width))],
        out_specs=at_k(width),
        out_shape=shaped(seqs, tokens, width),
        name="inner",
    )(
        prompt_x,
        prompt_b,
        prompt_c,
        prompt_step,
        run,
        jnp.repeat(skip_weight, width // heads)[None],
    )
    chips = zx // 4
    pieces = pl.pallas_call(
        lambda *refs: pair_kernel(p2, heads, *refs),
        grid=(4,),
        in_specs=[
            pl.BlockSpec(memory_space=pltpu.SMEM),
            pl.BlockSpec((seqs, chips * rows, n), lambda j: (0, j, 0)),
            full((seqs, 8, n)),
            pl.BlockSpec((seqs, chips * rows, n), lambda j: (0, j, 0)),
            pl.BlockSpec((seqs, 8, n), lambda j: (0, half // 8, 0)),
        ],
        out_specs=pl.BlockSpec((chips, 2 * rows + 8, n), lambda j: (j, 0, 0)),
        out_shape=shaped(zx, 2 * rows + 8, n),
        name="pair",
    )(core, keep, logs, came, came)
    pieces = lax.all_to_all(pieces, ZX, 0, 0, tiled=True)
    table = shaped(rows, many)
    grow, xs, add = call(
        lambda *refs: tables_kernel(p2, heads, *refs),
        (table, table, table),
        c_q,
        b_q,
        cum_q,
        x_q,
        step_q,
        skip_col,
    )
    enter, step_y, last = call(
        lambda *refs: scan_kernel(p2, heads, *refs),
        (shaped(zx, 2 * rows, n), shaped(grp, rows, many), shaped(2 * rows, n)),
        pieces,
        c_q,
        grow,
        add,
    )
    row_state = call(rows_kernel, shaped(decode_rows, rows, n), last, b_q, grow, xs)
    decode_state = row_state.reshape(decode_rows, heads, p2, n)

    ys = lax.all_to_all(step_y, GRP, 0, 0, tiled=True)
    partial = call(
        lambda *refs: project_kernel(ny, nxh, *refs),
        shaped(many, wide),
        place,
        ys,
        swapped(ys),
        *w_own,
        smem=(0,),
    )
    partial = lax.all_to_all(partial.reshape(zx, many // zx, wide), ZX, 0, 0, tiled=True)
    summed = jnp.sum(partial, axis=0)
    own_cols = told(summed, ZX).reshape(many, wide)
    blocks_y = []
    for dx in range(nxh):
        across = own_cols
        if dx:
            across = lax.ppermute(own_cols, XH, [(i, (i + dx) % nxh) for i in range(nxh)])
        for dy in range(ny):
            shift = [(i, (i + dy) % ny) for i in range(ny)]
            blocks_y.append((dy, dx, lax.ppermute(across, Y, shift) if dy else across))
    steps_y = [(dy, dx) for dy, dx, _ in blocks_y]
    own_half = [value for *_, value in blocks_y]
    other_half = [swapped(value) for value in own_half]
    enter, _ = lax.optimization_barrier((enter, own_cols))

    parts = call(
        lambda *refs: logits_kernel(ny, nxh, steps_y, *refs),
        shaped(size_of((Z, CO)), 3, many),
        place,
        *own_half,
        *other_half,
        norm_gain[None],
        lm_head,
        allowed,
        chosen_q,
        smem=(0,),
    )
    parts = lax.all_to_all(parts, (Z, CO), 0, 0, tiled=True)
    parts = jnp.stack(merge(parts))
    parts = told(parts, (XL, Y, XH))
    top, total, picked = merge(parts)
    logprob = picked - top - jnp.log(total)
    logprob = logprob.reshape(seqs, STEPS, per).transpose(1, 0, 2).reshape(STEPS, decode_rows)

    back = lax.all_to_all(enter, ZX, 0, 0, tiled=True).reshape(zx, seqs, rows, n)
    is_first = core[0] == 0

    def after(log_row, value, state):
        fade = jnp.exp(jnp.repeat(log_row[:, 0, :heads], p2, axis=1))[None, :, :, None]
        state = state[:, :half].reshape(seqs, zx, rows, n).transpose(1, 0, 2, 3)
        return fade * value + state

    for_me = jnp.where(is_first, back, after(came[:, half:], back, came))
    for_other = jnp.where(is_first, after(logs[:, 4:], back, keep), back)
    other_side = swapped(for_other)

    assert blocks == 2
    prompt_y = ()
    for s in range(seqs):
        of_s = lambda *shape, s=s: pl.BlockSpec((1, *shape), lambda _: (s,) + (0,) * len(shape))
        states_s = pl.BlockSpec((zx, 1, rows, n), lambda _, s=s: (0, s, 0, 0))
        prompt_y = pl.pallas_call(
            lambda *refs: carry_kernel(zx, p2, heads, *refs),
            grid=(1,),
            in_specs=[
                pl.BlockSpec(memory_space=pltpu.SMEM),
                of_s(tokens, width),
                of_s(tokens, n),
                of_s(heads, tokens),
                of_s(8, n),
                states_s,
                states_s,
                of_s(width, n),
                *[pl.BlockSpec(memory_space=pl.ANY) for _ in prompt_y],
            ],
            out_specs=of_s(tokens, width),
            out_shape=shaped(seqs, tokens, width, dtype=BF16),
            input_output_aliases={8: 0} if prompt_y else {},
            scratch_shapes=[pltpu.VMEM((width, width), BF16)],
        )(core, inner, prompt_c, run, logs, for_me, other_side, e0, *prompt_y)
        prompt_y = (prompt_y,)
    (prompt_y,) = prompt_y
    return (prompt_y, decode_state, logprob)


def solution(mesh):
    ctx, grp = mesh.devices.shape
    shape = (ctx // 4, 2, 2, grp // 2, 2)
    finer = Mesh(mesh.devices.reshape(shape), ALL)
    in_specs = (
        P(None, CTX, GRP),
        P(None, CTX, GRP),
        P(None, CTX, GRP),
        P(None, GRP, CTX),
        P(None, GRP, CTX),
        P(GRP),
        P(None, None, GRP, CTX),
        P(None, None, GRP),
        P(None, None, GRP),
        P(None, None, GRP),
        P(None, None, GRP),
        P(GRP, CTX, None),
        P(),
        P(None, ALL),
        P(None, ALL),
        P(),
        P(),
    )
    out_specs = (P(None, CTX, GRP), P(None, GRP, CTX, None), P())

    return jax.shard_map(body, mesh=finer, in_specs=in_specs, out_specs=out_specs, check_vma=False)
```

```python
import jax
import jax.numpy as jnp
import numpy as np
from jax import lax
from jax.experimental import pallas as pl
from jax.experimental.pallas import tpu as pltpu
from jax.sharding import Mesh
from jax.sharding import PartitionSpec as P


BLOCK = 256
STEPS = 4
Z, XL, CO, Y, XH = "z", "xl", "co", "y", "xh"
CTX = (Z, XL, CO)
GRP = (Y, XH)
ALL = (Z, XL, CO, Y, XH)
ZX = (Z, XL)
CG = (CO, Y, XH)

NEG_BIG = -1e30
EPS = 1e-05
F32 = jnp.float32
BF16 = jnp.bfloat16
HI = lax.Precision.HIGHEST


def size_of(axes):
    return int(np.prod([lax.axis_size(a) for a in axes]))


def iota(shape, dim):
    return lax.broadcasted_iota(jnp.int32, shape, dim)


def dot(a, b, dims, precision=None):
    return lax.dot_general(a, b, (dims, ((), ())), precision=precision, preferred_element_type=F32)


def in_thirds(value, axis):
    high = value.astype(BF16)
    rest = value - high.astype(F32)
    middle = rest.astype(BF16)
    low = (rest - middle.astype(F32)).astype(BF16)
    return jnp.concatenate([high, middle, low], axis=axis)


def one_hot_thirds(shape, axis, match):
    return jnp.concatenate([match(shape).astype(BF16)] * 3, axis=axis)


def expander(heads, width):
    per = width // heads
    return one_hot_thirds(
        (heads, width), 0, lambda shape: iota(shape, 1) // per == iota(shape, 0)
    )


def swapped(value):
    return lax.ppermute(value, CO, [(0, 1), (1, 0)])


def told(value, axes):
    many = size_of(axes)
    return lax.all_to_all(
        jnp.broadcast_to(value[None], (many, *value.shape)), axes, 0, 0, tiled=True
    )


def column(row, rows, per):
    width = row.shape[1]
    pick = iota((rows, width), 1) == iota((rows, width), 0) // per
    return jnp.sum(jnp.where(pick, row, 0.0), axis=1, keepdims=True)


def local_index(feature, my_core, head_dim, zx, p2, heads):
    h, p = feature // head_dim, feature % head_dim
    chip, rest = p // (2 * p2), p % (2 * p2)
    side = (rest // p2) ^ my_core
    return ((side * zx + chip) * heads + h) * p2 + rest % p2


def states_kernel(zx, p2, core, x, b, step, decay, e0, keep, send, run_out, logs, perm_t):
    tokens, width = x.shape[1], x.shape[2]
    heads = step.shape[1]
    head_dim = width // heads
    half = width // 2
    blocks = tokens // BLOCK

    @pl.when(pl.program_id(0) == 0)
    def _():
        goes = local_index(iota((1, width), 1), core[0], head_dim, zx, p2, heads)
        perm_t[...] = (iota((width, width), 0) == goes).astype(BF16)

    upper = (iota((BLOCK, BLOCK), 0) <= iota((BLOCK, BLOCK), 1)).astype(BF16)
    of_row = one_hot_thirds(
        (width, heads), 1, lambda shape: iota(shape, 0) // p2 % heads == iota(shape, 1)
    )
    lane = iota((heads, BLOCK), 1) == iota((heads, BLOCK), 0)
    total_row = jnp.zeros((1, BLOCK), F32)
    to_end, totals = [], []
    for k in range(blocks):
        at = slice(k * BLOCK, (k + 1) * BLOCK)
        run = dot(in_thirds(decay[0, :, at], 0), upper, ((1,), (0,)))
        run = run[:heads] + run[heads : 2 * heads] + run[2 * heads :]
        run_out[0, :, at] = run
        total = jnp.broadcast_to(run[:, BLOCK - 1 :], (heads, BLOCK))
        to_end.append(step[0, :, at] * jnp.exp(total - run))
        totals.append(total)
        total_row = total_row + jnp.sum(jnp.where(lane, total, 0.0), axis=0, keepdims=True)
        if k == 0:
            logs[0, :4] = jnp.broadcast_to(total_row, (4, BLOCK))
    logs[0, 4:] = jnp.broadcast_to(total_row, (4, BLOCK))
    send[0, half:] = jnp.broadcast_to(total_row, (8, BLOCK))
    ends = in_thirds(jnp.concatenate(to_end, axis=1).T, 1)
    spread = dot(ends, expander(heads, width), ((1,), (0,)))
    scaled = (x[0].astype(F32) * spread).astype(BF16)
    moved = dot(perm_t[...], scaled, ((1,), (1,))).astype(BF16)
    state = None
    for k in range(blocks):
        at = slice(k * BLOCK, (k + 1) * BLOCK)
        own = dot(moved[:, at], b[0, at], ((1,), (0,)))
        if k == 0:
            state = own
            e0[0] = own
        else:
            fade = dot(of_row, in_thirds(jnp.exp(totals[k]), 0), ((1,), (0,)))
            state = fade * state + own
    keep[0] = state[:half]
    send[0, :half] = state[half:]


def pair_kernel(p2, heads, core, keep, logs, came, out):
    rows = heads * p2
    first = core[0] == 0
    for s in range(keep.shape[0]):
        mine = logs[s, 4:5]
        other = came[s, keep.shape[1] : keep.shape[1] + 1]
        f_mine = jnp.where(first, jnp.exp(column(other, rows, p2)), 1.0)
        f_came = jnp.where(first, 1.0, jnp.exp(column(mine, rows, p2)))
        for k in range(keep.shape[1] // rows):
            at = slice(k * rows, (k + 1) * rows)
            out[k, s * rows : (s + 1) * rows] = f_mine * keep[s, at] + f_came * came[s, at]
            out[k, 2 * rows + s * 4 : 2 * rows + s * 4 + 4] = jnp.broadcast_to(
                mine + other, (4, mine.shape[1])
            )


def tables_kernel(p2, heads, c_q, b_q, cum, x_q, step_q, skip_col, grow, xs, add):
    rows, many = x_q.shape
    half = many // 2
    per = half // STEPS
    repeat = (iota((rows, heads), 0) // p2 == iota((rows, heads), 1)).astype(F32)
    cums = dot(repeat, cum[...], ((1,), (0,)), HI)
    steps = dot(repeat, step_q[...], ((1,), (0,)), HI)
    growth = jnp.exp(cums)
    inject = x_q[...] * steps * jnp.exp(-cums)
    cross = dot(b_q[...], c_q[...], ((1,), (1,)))
    earlier, later = iota((many, many), 0), iota((many, many), 1)
    same = (earlier // half == later // half) & (earlier % per == later % per)
    cross = jnp.where(same & (earlier <= later), cross, 0.0)
    grow[...] = growth
    xs[...] = inject
    add[...] = growth * dot(inject, cross, ((1,), (0,)), HI) + skip_col[...] * x_q[...]


def scan_kernel(p2, heads, pieces, c_q, grow, add, enter, step_y, last):
    zx = pieces.shape[0]
    rows = heads * p2
    many = c_q.shape[0]
    final = jnp.zeros((2 * rows, pieces.shape[2]), F32)
    for k in range(zx):
        enter[k] = final
        fac = jnp.concatenate(
            [
                jnp.exp(column(pieces[k, 2 * rows + 4 * s : 2 * rows + 4 * s + 1], rows, p2))
                for s in range(2)
            ],
            axis=0,
        )
        final = fac * final + pieces[k, : 2 * rows]
    last[...] = final
    seen = dot(final, c_q[...].astype(F32), ((1,), (1,)), HI)
    lane = iota((rows, many), 1)
    seen = jnp.where(lane < many // 2, seen[:rows], seen[rows:])
    y = grow[...] * seen + add[...]
    step_y[...] = jnp.broadcast_to(y.astype(BF16).astype(F32), step_y.shape)


def rows_kernel(last, b_q, grow, xs, row_state):
    rows, many = xs.shape
    half = many // 2
    per = half // STEPS
    b_all = b_q[...].astype(F32)
    growth, inject = grow[...], xs[...]
    for s in range(2):
        for r in range(per):
            value = last[s * rows : (s + 1) * rows]
            for i in range(STEPS):
                q = s * half + i * per + r
                value = value + inject[:, q : q + 1] * b_all[q : q + 1]
            row_state[s * per + r] = growth[:, q : q + 1] * value


def project_kernel(ny, nxh, own, other, *refs):
    pieces, out = refs[:-1], refs[-1]
    iy, ixh = lax.axis_index(Y), lax.axis_index(XH)
    left, right = [], []
    for number, piece in enumerate(pieces):
        dy, dx = number // nxh, number % nxh
        at = lax.rem(iy + (ny - dy), ny) * nxh + lax.rem(ixh + (nxh - dx), nxh)
        left += [own[at], other[at]]
        right.append(piece[...].reshape(-1, piece.shape[2]))
    left = jnp.concatenate(left, axis=0).T.astype(BF16)
    right = jnp.concatenate(right, axis=0).astype(BF16)
    out[...] = dot(left, right, ((1,), (0,)))


def logits_kernel(ny, nxh, steps, *refs):
    number = 2 * len(steps)
    arrays = refs[:number]
    gain, head, allowed, chosen, out, got, weights, sems = refs[number:]
    many, width = arrays[0].shape
    model = head.shape[0]
    core, iy, ixh = (lax.axis_index(a) for a in (CO, Y, XH))
    starts, waits = [], []
    for j, ref in enumerate(arrays):
        dy, dx = steps[j // 2]
        of_y = lax.rem(iy + (ny - dy), ny)
        of_x = lax.rem(ixh + (nxh - dx), nxh)
        block = (((core + j % 2) % 2) * ny + of_y) * nxh + of_x
        starts.append(pl.multiple_of(block * width, width))
        pair = (
            pltpu.make_async_copy(ref, got.at[j], sems.at[2 * j]),
            pltpu.make_async_copy(
                head.at[pl.ds(starts[j], width)], weights.at[j], sems.at[2 * j + 1]
            ),
        )
        for copy in pair:
            copy.start()
        waits.append(pair)
    squares = jnp.zeros((many, 128), F32)
    acc = jnp.zeros((many, head.shape[1]), F32)
    for j in range(number):
        for copy in waits[j]:
            copy.wait()
        part = got[j]
        scaled = (part * gain[:, pl.ds(starts[j], width)]).astype(BF16)
        acc = acc + dot(scaled, weights[j], ((1,), (0,)))
        part = part * part
        for k in range(width // 128):
            squares = squares + part[:, k * 128 : (k + 1) * 128]
    acc = acc * lax.rsqrt(jnp.sum(squares, axis=1, keepdims=True) / model + EPS)
    acc = acc.T
    ok = allowed[...] > 0.5
    top = jnp.max(jnp.where(ok, acc, NEG_BIG), axis=0, keepdims=True)
    total = jnp.sum(jnp.where(ok, jnp.exp(acc - top), 0.0), axis=0, keepdims=True)
    hit = iota(acc.shape, 0) == chosen[...]
    picked = jnp.sum(jnp.where(hit, acc, 0.0), axis=0, keepdims=True)
    out[...] = jnp.broadcast_to(jnp.concatenate([top, total, picked], axis=0)[None], out.shape)


def inner_kernel(x, b, c, step, run, skip, out):
    width = x.shape[2]
    heads = step.shape[1]
    head_dim = width // heads
    xb = x[0]
    running, steps = run[0], step[0]
    run_t = running.T
    causal = iota((BLOCK, BLOCK), 1) <= iota((BLOCK, BLOCK), 0)
    scores = jnp.where(causal, dot(c[0], b[0], ((1,), (1,))), 0.0)
    pair = 2 * head_dim
    left = iota((BLOCK, pair), 1) < head_dim
    for j in range(heads // 2):
        at = slice(j * pair, (j + 1) * pair)
        halves = []
        for h in (2 * j, 2 * j + 1):
            gap = jnp.minimum(run_t[:, h : h + 1] - running[h : h + 1], 0.0)
            mix = (scores * jnp.exp(gap) * steps[h : h + 1]).astype(BF16)
            halves.append(dot(mix, xb[:, at], ((1,), (0,))))
        inner = jnp.where(left, halves[0], halves[1])
        out[0, :, at] = inner + skip[:, at] * xb[:, at].astype(F32)


def carry_kernel(
    zx, p2, heads, core, inner, c, run, logs, own, other, came, came_log, kept, e0, *refs
):
    out, both = refs[-2:]
    width = inner.shape[2]
    head_dim = width // heads
    rows = heads * p2

    @pl.when(pl.program_id(0) == 0)
    def _():
        goes = local_index(iota((width, 1), 0), core[0], head_dim, zx, p2, heads)
        perm = (iota((width, width), 1) == goes).astype(BF16)
        enter = jnp.concatenate(
            [own[:, 0].reshape(zx * rows, -1), other[:, 0].reshape(zx * rows, -1)], axis=0
        )
        n = enter.shape[1]
        second = core[0] == 1
        past = jnp.exp(jnp.where(second, column(came_log[0, :1], rows, p2), 0.0))
        before = jnp.where(second, jnp.concatenate([came[0], kept[0]], axis=0), 0.0)
        enter = (enter.reshape(2 * zx, rows, n) * past[None]).reshape(width, n) + before
        fade = jnp.exp(column(logs[0, :1], rows, p2))
        after = (enter.reshape(2 * zx, rows, n) * fade[None]).reshape(width, n) + e0[0]
        for k, value in enumerate((enter, after)):
            both[k] = dot(perm, value.astype(BF16), ((1,), (0,))).astype(BF16)

    growth = dot(in_thirds(jnp.exp(run[0].T), 1), expander(heads, width), ((1,), (0,)))
    carry = dot(c[0], both[pl.program_id(0)], ((1,), (1,)))
    out[0] = (inner[0] + growth * carry).astype(BF16)


def merge(parts):
    top = jnp.max(parts[:, 0], axis=0)
    total = jnp.sum(parts[:, 1] * jnp.exp(parts[:, 0] - top), axis=0)
    picked = jnp.sum(parts[:, 2], axis=0)
    return top, total, picked


def full(shape):
    return pl.BlockSpec(shape, lambda *_: (0,) * len(shape))


def call(kernel, outs, *args, smem=(), anywhere=()):
    def spec(k, arg):
        if k in smem:
            return pl.BlockSpec(memory_space=pltpu.SMEM)
        if k in anywhere:
            return pl.BlockSpec(memory_space=pl.ANY)
        return full(arg.shape)

    specs = [spec(k, arg) for k, arg in enumerate(args)]
    many = isinstance(outs, tuple)
    return pl.pallas_call(
        kernel,
        grid=(1,),
        in_specs=specs,
        out_specs=tuple(full(o.shape) for o in outs) if many else full(outs.shape),
        out_shape=outs,
    )(*args)


def shaped(*shape, dtype=F32):
    return jax.ShapeDtypeStruct(shape, dtype)


def body(
    prompt_x,
    prompt_b,
    prompt_c,
    prompt_step,
    prompt_decay,
    skip_weight,
    decode_x,
    decode_b,
    decode_c,
    decode_step,
    decode_decay,
    out_proj,
    norm_gain,
    lm_head,
    mask_words,
    state_ids,
    chosen,
):
    seqs, tokens, width = prompt_x.shape
    n = prompt_b.shape[2]
    heads = prompt_step.shape[1]
    zx, cg, grp = size_of(ZX), size_of(CG), size_of(GRP)
    p2 = decode_x.shape[3]
    rows = heads * p2
    half = width // 2
    blocks = tokens // BLOCK
    decode_rows = decode_x.shape[1]
    per = decode_rows // seqs
    many = STEPS * decode_rows
    core = lax.axis_index(CO).astype(jnp.int32)[None]

    model = out_proj.shape[2]
    wide = model // cg
    ny, nxh = lax.axis_size(Y), lax.axis_size(XH)
    iy, ixh = (lax.axis_index(a).astype(jnp.int32) for a in (Y, XH))
    grp_steps = [(dy, dx) for dy in range(ny) for dx in range(nxh)]

    def grp_perm(dy, dx):
        return [
            (y * nxh + x, (y + dy) % ny * nxh + (x + dx) % nxh)
            for y in range(ny)
            for x in range(nxh)
        ]

    w_rows = out_proj.astype(F32).reshape(rows, 2, grp, wide).transpose(1, 2, 0, 3)
    w_keep = lax.dynamic_index_in_dim(w_rows, core[0], 0, keepdims=False)
    w_other = lax.dynamic_index_in_dim(w_rows, 1 - core[0], 0, keepdims=False)
    w_came = swapped(w_other)
    w_both = jnp.stack([w_keep, w_came], axis=1)
    w_own = []
    for dy, dx in grp_steps:
        to = (iy + dy) % ny * nxh + (ixh + dx) % nxh
        part = lax.dynamic_index_in_dim(w_both, to, 0, keepdims=False)
        w_own.append(lax.ppermute(part, GRP, grp_perm(dy, dx)) if dy or dx else part)

    def by_q(value):
        shape = value.shape[2:]
        value = value.reshape(STEPS, seqs, per, *shape)
        return jnp.moveaxis(value, 1, 0).reshape(many, *shape)

    c_q, b_q = by_q(decode_c), by_q(decode_b)
    cum_q = by_q(jnp.cumsum(decode_decay, axis=0)).T
    step_q = by_q(decode_step).T
    x_q = by_q(decode_x.astype(F32).reshape(STEPS, decode_rows, rows)).T
    skip_col = jnp.repeat(skip_weight, p2)[:, None]
    vocab = lm_head.shape[1]
    first = (lax.axis_index(CTX) * size_of(GRP) + lax.axis_index(GRP)) * vocab
    chosen_q = (by_q(chosen) - first)[None]
    ids_q = by_q(state_ids)
    bits = (
        jnp.right_shift(mask_words[:, :, None], jnp.arange(32, dtype=jnp.int32)[None, None]) & 1
    ).reshape(mask_words.shape[0], vocab)
    onehot = (ids_q[None] == jnp.arange(mask_words.shape[0])[:, None]).astype(BF16)
    allowed = dot(bits.astype(BF16), onehot, ((0,), (0,)))

    by_s = lambda *shape: pl.BlockSpec((1, *shape), lambda s: (s,) + (0,) * len(shape))
    e0, keep, send, run, logs = pl.pallas_call(
        lambda *refs: states_kernel(zx, p2, *refs),
        grid=(seqs,),
        in_specs=[
            pl.BlockSpec(memory_space=pltpu.SMEM),
            by_s(tokens, width),
            by_s(tokens, n),
            by_s(heads, tokens),
            by_s(heads, tokens),
        ],
        out_specs=(
            by_s(width, n),
            by_s(half, n),
            by_s(half + 8, n),
            by_s(heads, tokens),
            by_s(8, n),
        ),
        out_shape=(
            shaped(seqs, width, n),
            shaped(seqs, half, n),
            shaped(seqs, half + 8, n),
            shaped(seqs, heads, tokens),
            shaped(seqs, 8, n),
        ),
        scratch_shapes=[pltpu.VMEM((width, width), BF16)],
        name="states",
    )(core, prompt_x, prompt_b, prompt_step, prompt_decay)
    at_k = lambda *shape: pl.BlockSpec((1, BLOCK, *shape), lambda s, k: (s, k, 0))
    lanes_k = pl.BlockSpec((1, heads, BLOCK), lambda s, k: (s, 0, k))
    came = swapped(send)
    inner = pl.pallas_call(
        inner_kernel,
        grid=(seqs, blocks),
        in_specs=[at_k(width), at_k(n), at_k(n), lanes_k, lanes_k, full((1, width))],
        out_specs=at_k(width),
        out_shape=shaped(seqs, tokens, width),
        name="inner",
    )(
        prompt_x,
        prompt_b,
        prompt_c,
        prompt_step,
        run,
        jnp.repeat(skip_weight, width // heads)[None],
    )
    pieces = pl.pallas_call(
        lambda *refs: pair_kernel(p2, heads, *refs),
        grid=(1,),
        in_specs=[
            pl.BlockSpec(memory_space=pltpu.SMEM),
            full((seqs, half, n)),
            full((seqs, 8, n)),
            full((seqs, half + 8, n)),
        ],
        out_specs=full((zx, 2 * rows + 8, n)),
        out_shape=shaped(zx, 2 * rows + 8, n),
        name="pair",
    )(core, keep, logs, came)
    kept_other = swapped(keep)
    pieces = lax.all_to_all(pieces, ZX, 0, 0, tiled=True)
    table = shaped(rows, many)
    grow, xs, add = call(
        lambda *refs: tables_kernel(p2, heads, *refs),
        (table, table, table),
        c_q,
        b_q,
        cum_q,
        x_q,
        step_q,
        skip_col,
    )
    enter, step_y, last = call(
        lambda *refs: scan_kernel(p2, heads, *refs),
        (shaped(zx, 2 * rows, n), shaped(grp, rows, many), shaped(2 * rows, n)),
        pieces,
        c_q,
        grow,
        add,
    )
    row_state = call(rows_kernel, shaped(decode_rows, rows, n), last, b_q, grow, xs)
    decode_state = row_state.reshape(decode_rows, heads, p2, n)

    ys = lax.all_to_all(step_y, GRP, 0, 0, tiled=True)
    partial = call(
        lambda *refs: project_kernel(ny, nxh, *refs), shaped(many, wide), ys, swapped(ys), *w_own
    )
    partial = lax.all_to_all(partial.reshape(zx, many // zx, wide), ZX, 0, 0, tiled=True)
    summed = jnp.sum(partial, axis=0)
    own_cols = told(summed, ZX).reshape(many, wide)
    assert ny == 4 and nxh == 2

    def moved_y(value, by):
        return lax.ppermute(value, Y, [(i, (i + by) % ny) for i in range(ny)])

    up, down = moved_y(own_cols, 1), moved_y(own_cols, 3)
    across = lax.ppermute(own_cols, XH, [(0, 1), (1, 0)])
    up_2 = moved_y(up, 1)
    across_up, across_down = moved_y(across, 1), moved_y(across, 3)
    across_2 = moved_y(across_down, 3)
    blocks_y = [
        (0, 0, own_cols),
        (1, 0, up),
        (3, 0, down),
        (0, 1, across),
        (2, 0, up_2),
        (1, 1, across_up),
        (3, 1, across_down),
        (2, 1, across_2),
    ]
    steps_y = [(dy, dx) for dy, dx, _ in blocks_y]
    own_half = [value for *_, value in blocks_y]
    other_half = [swapped(value) for value in own_half]
    enter, _ = lax.optimization_barrier((enter, own_cols))

    halves = [value for pair in zip(own_half, other_half) for value in pair]
    anywhere = pl.BlockSpec(memory_space=pl.ANY)
    parts_shape = (size_of((Z, CO)), 3, many)
    parts = pl.pallas_call(
        lambda *refs: logits_kernel(ny, nxh, steps_y, *refs),
        grid=(1,),
        in_specs=[anywhere] * len(halves)
        + [full((1, model)), anywhere, full(allowed.shape), full(chosen_q.shape)],
        out_specs=full(parts_shape),
        out_shape=shaped(*parts_shape),
        scratch_shapes=[
            pltpu.VMEM((len(halves), many, wide), F32),
            pltpu.VMEM((len(halves), wide, vocab), BF16),
            pltpu.SemaphoreType.DMA((2 * len(halves),)),
        ],
        name="logits",
    )(*halves, norm_gain[None], lm_head, allowed, chosen_q)
    parts = lax.all_to_all(parts, (Z, CO), 0, 0, tiled=True)
    parts = jnp.stack(merge(parts))
    parts = told(parts, (XL, Y, XH))
    top, total, picked = merge(parts)
    logprob = picked - top - jnp.log(total)
    logprob = logprob.reshape(seqs, STEPS, per).transpose(1, 0, 2).reshape(STEPS, decode_rows)

    back = lax.all_to_all(enter, ZX, 0, 0, tiled=True).reshape(zx, seqs, rows, n)
    back_other = swapped(back)
    prompt_y = ()
    for s in range(seqs):
        of_s = lambda *shape, s=s: pl.BlockSpec((1, *shape), lambda k: (s,) + (0,) * len(shape))
        at_k = lambda *shape, s=s: pl.BlockSpec((1, BLOCK, *shape), lambda k: (s, k, 0))
        lanes_k = pl.BlockSpec((1, heads, BLOCK), lambda k, s=s: (s, 0, k))
        states_s = pl.BlockSpec((zx, 1, rows, n), lambda k, s=s: (0, s, 0, 0))
        prompt_y = pl.pallas_call(
            lambda *refs: carry_kernel(zx, p2, heads, *refs),
            grid=(blocks,),
            in_specs=[
                pl.BlockSpec(memory_space=pltpu.SMEM),
                at_k(width),
                at_k(n),
                lanes_k,
                of_s(8, n),
                states_s,
                states_s,
                of_s(half, n),
                pl.BlockSpec((1, 8, n), lambda k, s=s: (s, half // 8, 0)),
                of_s(half, n),
                of_s(width, n),
                *[pl.BlockSpec(memory_space=pl.ANY) for _ in prompt_y],
            ],
            out_specs=at_k(width),
            out_shape=shaped(seqs, tokens, width, dtype=BF16),
            input_output_aliases={11: 0} if prompt_y else {},
            scratch_shapes=[pltpu.VMEM((blocks, width, n), BF16)],
        )(core, inner, prompt_c, run, logs, back, back_other, came, came, kept_other, e0, *prompt_y)
        prompt_y = (prompt_y,)
    (prompt_y,) = prompt_y
    return (prompt_y, decode_state, logprob)


def solution(mesh):
    ctx, grp = mesh.devices.shape
    shape = (ctx // 4, 2, 2, grp // 2, 2)
    finer = Mesh(mesh.devices.reshape(shape), ALL)
    in_specs = (
        P(None, CTX, GRP),
        P(None, CTX, GRP),
        P(None, CTX, GRP),
        P(None, GRP, CTX),
        P(None, GRP, CTX),
        P(GRP),
        P(None, None, GRP, CTX),
        P(None, None, GRP),
        P(None, None, GRP),
        P(None, None, GRP),
        P(None, None, GRP),
        P(GRP, CTX, None),
        P(),
        P(None, ALL),
        P(None, ALL),
        P(),
        P(),
    )
    out_specs = (P(None, CTX, GRP), P(None, GRP, CTX, None), P())

    return jax.shard_map(body, mesh=finer, in_specs=in_specs, out_specs=out_specs, check_vma=False)
```

```python
import jax
import jax.numpy as jnp
import numpy as np
from jax import lax
from jax.experimental import pallas as pl
from jax.experimental.pallas import tpu as pltpu
from jax.sharding import Mesh
from jax.sharding import PartitionSpec as P


BLOCK = 256
STEPS = 4
Z, XL, CO, Y, XH = "z", "xl", "co", "y", "xh"
CTX = (Z, XL, CO)
GRP = (Y, XH)
ALL = (Z, XL, CO, Y, XH)
ZX = (Z, XL)
CG = (CO, Y, XH)

ROOM = pltpu.CompilerParams(vmem_limit_bytes=24 * 2**20)

NEG_BIG = -1e30
EPS = 1e-05
F32 = jnp.float32
BF16 = jnp.bfloat16
HI = lax.Precision.HIGHEST


def size_of(axes):
    return int(np.prod([lax.axis_size(a) for a in axes]))


def iota(shape, dim):
    return lax.broadcasted_iota(jnp.int32, shape, dim)


def dot(a, b, dims, precision=None):
    return lax.dot_general(a, b, (dims, ((), ())), precision=precision, preferred_element_type=F32)


def in_thirds(value, axis):
    high = value.astype(BF16)
    rest = value - high.astype(F32)
    middle = rest.astype(BF16)
    low = (rest - middle.astype(F32)).astype(BF16)
    return jnp.concatenate([high, middle, low], axis=axis)


def one_hot_thirds(shape, axis, match):
    return jnp.concatenate([match(shape).astype(BF16)] * 3, axis=axis)


def expander(heads, width):
    per = width // heads
    return one_hot_thirds(
        (heads, width), 0, lambda shape: iota(shape, 1) // per == iota(shape, 0)
    )


def swapped(value):
    return lax.ppermute(value, CO, [(0, 1), (1, 0)])


def told(value, axes):
    many = size_of(axes)
    return lax.all_to_all(
        jnp.broadcast_to(value[None], (many, *value.shape)), axes, 0, 0, tiled=True
    )


def column(row, rows, per):
    width = row.shape[1]
    pick = iota((rows, width), 1) == iota((rows, width), 0) // per
    return jnp.sum(jnp.where(pick, row, 0.0), axis=1, keepdims=True)


def local_index(feature, my_core, head_dim, zx, p2, heads):
    h, p = feature // head_dim, feature % head_dim
    chip, rest = p // (2 * p2), p % (2 * p2)
    side = (rest // p2) ^ my_core
    return ((side * zx + chip) * heads + h) * p2 + rest % p2


def states_kernel(zx, p2, core, x, b, step, decay, e0, keep, send, run_out, logs, perm_t):
    tokens, width = x.shape[1], x.shape[2]
    heads = step.shape[1]
    head_dim = width // heads
    half = width // 2
    blocks = tokens // BLOCK

    @pl.when(pl.program_id(0) == 0)
    def _():
        goes = local_index(iota((1, width), 1), core[0], head_dim, zx, p2, heads)
        perm_t[...] = (iota((width, width), 0) == goes).astype(BF16)

    upper = (iota((BLOCK, BLOCK), 0) <= iota((BLOCK, BLOCK), 1)).astype(BF16)
    of_row = one_hot_thirds(
        (width, heads), 1, lambda shape: iota(shape, 0) // p2 % heads == iota(shape, 1)
    )
    lane = iota((heads, BLOCK), 1) == iota((heads, BLOCK), 0)
    total_row = jnp.zeros((1, BLOCK), F32)
    to_end, totals = [], []
    for k in range(blocks):
        at = slice(k * BLOCK, (k + 1) * BLOCK)
        run = dot(in_thirds(decay[0, :, at], 0), upper, ((1,), (0,)))
        run = run[:heads] + run[heads : 2 * heads] + run[2 * heads :]
        run_out[0, :, at] = run
        total = jnp.broadcast_to(run[:, BLOCK - 1 :], (heads, BLOCK))
        to_end.append(step[0, :, at] * jnp.exp(total - run))
        totals.append(total)
        total_row = total_row + jnp.sum(jnp.where(lane, total, 0.0), axis=0, keepdims=True)
        if k == 0:
            logs[0, :4] = jnp.broadcast_to(total_row, (4, BLOCK))
    logs[0, 4:] = jnp.broadcast_to(total_row, (4, BLOCK))
    send[0, half:] = jnp.broadcast_to(total_row, (8, BLOCK))
    ends = in_thirds(jnp.concatenate(to_end, axis=1).T, 1)
    spread = dot(ends, expander(heads, width), ((1,), (0,)))
    scaled = (x[0].astype(F32) * spread).astype(BF16)
    moved = dot(perm_t[...], scaled, ((1,), (1,))).astype(BF16)
    state = None
    for k in range(blocks):
        at = slice(k * BLOCK, (k + 1) * BLOCK)
        own = dot(moved[:, at], b[0, at], ((1,), (0,)))
        if k == 0:
            state = own
            e0[0] = own
        else:
            fade = dot(of_row, in_thirds(jnp.exp(totals[k]), 0), ((1,), (0,)))
            state = fade * state + own
    keep[0] = state[:half]
    send[0, :half] = state[half:]


def pair_kernel(p2, heads, core, keep, logs, came, out):
    rows = heads * p2
    first = core[0] == 0
    for s in range(keep.shape[0]):
        mine = logs[s, 4:5]
        other = came[s, keep.shape[1] : keep.shape[1] + 1]
        f_mine = jnp.where(first, jnp.exp(column(other, rows, p2)), 1.0)
        f_came = jnp.where(first, 1.0, jnp.exp(column(mine, rows, p2)))
        for k in range(keep.shape[1] // rows):
            at = slice(k * rows, (k + 1) * rows)
            out[k, s * rows : (s + 1) * rows] = f_mine * keep[s, at] + f_came * came[s, at]
            out[k, 2 * rows + s * 4 : 2 * rows + s * 4 + 4] = jnp.broadcast_to(
                mine + other, (4, mine.shape[1])
            )


def tables_kernel(p2, heads, c_q, b_q, cum, x_q, step_q, skip_col, grow, xs, add):
    rows, many = x_q.shape
    half = many // 2
    per = half // STEPS
    repeat = (iota((rows, heads), 0) // p2 == iota((rows, heads), 1)).astype(F32)
    cums = dot(repeat, cum[...], ((1,), (0,)), HI)
    steps = dot(repeat, step_q[...], ((1,), (0,)), HI)
    growth = jnp.exp(cums)
    inject = x_q[...] * steps * jnp.exp(-cums)
    cross = dot(b_q[...], c_q[...], ((1,), (1,)))
    earlier, later = iota((many, many), 0), iota((many, many), 1)
    same = (earlier // half == later // half) & (earlier % per == later % per)
    cross = jnp.where(same & (earlier <= later), cross, 0.0)
    grow[...] = growth
    xs[...] = inject
    add[...] = growth * dot(inject, cross, ((1,), (0,)), HI) + skip_col[...] * x_q[...]


def scan_kernel(p2, heads, pieces, c_q, grow, add, enter, step_y, last):
    zx = pieces.shape[0]
    rows = heads * p2
    many = c_q.shape[0]
    final = jnp.zeros((2 * rows, pieces.shape[2]), F32)
    for k in range(zx):
        enter[k] = final
        fac = jnp.concatenate(
            [
                jnp.exp(column(pieces[k, 2 * rows + 4 * s : 2 * rows + 4 * s + 1], rows, p2))
                for s in range(2)
            ],
            axis=0,
        )
        final = fac * final + pieces[k, : 2 * rows]
    last[...] = final
    seen = dot(final, c_q[...].astype(F32), ((1,), (1,)), HI)
    lane = iota((rows, many), 1)
    seen = jnp.where(lane < many // 2, seen[:rows], seen[rows:])
    y = grow[...] * seen + add[...]
    step_y[...] = jnp.broadcast_to(y.astype(BF16).astype(F32), step_y.shape)


def rows_kernel(last, b_q, grow, xs, row_state):
    rows, many = xs.shape
    half = many // 2
    per = half // STEPS
    b_all = b_q[...].astype(F32)
    growth, inject = grow[...], xs[...]
    for s in range(2):
        for r in range(per):
            value = last[s * rows : (s + 1) * rows]
            for i in range(STEPS):
                q = s * half + i * per + r
                value = value + inject[:, q : q + 1] * b_all[q : q + 1]
            row_state[s * per + r] = growth[:, q : q + 1] * value


def project_kernel(ny, nxh, own, other, *refs):
    pieces, out = refs[:-1], refs[-1]
    iy, ixh = lax.axis_index(Y), lax.axis_index(XH)
    left, right = [], []
    for number, piece in enumerate(pieces):
        dy, dx = number // nxh, number % nxh
        at = lax.rem(iy + (ny - dy), ny) * nxh + lax.rem(ixh + (nxh - dx), nxh)
        left += [own[at], other[at]]
        right.append(piece[...].reshape(-1, piece.shape[2]))
    left = jnp.concatenate(left, axis=0).T.astype(BF16)
    right = jnp.concatenate(right, axis=0).astype(BF16)
    out[...] = dot(left, right, ((1,), (0,)))


def logits_kernel(ny, nxh, steps, *refs):
    number = 2 * len(steps)
    arrays = refs[:number]
    gain, head, allowed, chosen, out, got, weights, sems = refs[number:]
    many, width = arrays[0].shape
    model = head.shape[0]
    core, iy, ixh = (lax.axis_index(a) for a in (CO, Y, XH))
    starts, waits = [], []
    for j, ref in enumerate(arrays):
        dy, dx = steps[j // 2]
        of_y = lax.rem(iy + (ny - dy), ny)
        of_x = lax.rem(ixh + (nxh - dx), nxh)
        block = (((core + j % 2) % 2) * ny + of_y) * nxh + of_x
        starts.append(pl.multiple_of(block * width, width))
        pair = (
            pltpu.make_async_copy(ref, got.at[j], sems.at[2 * j]),
            pltpu.make_async_copy(
                head.at[pl.ds(starts[j], width)], weights.at[j], sems.at[2 * j + 1]
            ),
        )
        for copy in pair:
            copy.start()
        waits.append(pair)
    squares = jnp.zeros((many, 128), F32)
    acc = jnp.zeros((many, head.shape[1]), F32)
    for j in range(number):
        for copy in waits[j]:
            copy.wait()
        part = got[j]
        scaled = (part * gain[:, pl.ds(starts[j], width)]).astype(BF16)
        acc = acc + dot(scaled, weights[j], ((1,), (0,)))
        part = part * part
        for k in range(width // 128):
            squares = squares + part[:, k * 128 : (k + 1) * 128]
    acc = acc * lax.rsqrt(jnp.sum(squares, axis=1, keepdims=True) / model + EPS)
    acc = acc.T
    ok = allowed[...] > 0.5
    top = jnp.max(jnp.where(ok, acc, NEG_BIG), axis=0, keepdims=True)
    total = jnp.sum(jnp.where(ok, jnp.exp(acc - top), 0.0), axis=0, keepdims=True)
    hit = iota(acc.shape, 0) == chosen[...]
    picked = jnp.sum(jnp.where(hit, acc, 0.0), axis=0, keepdims=True)
    out[...] = jnp.broadcast_to(jnp.concatenate([top, total, picked], axis=0)[None], out.shape)


def inner_kernel(x, b, c, step, run, skip, out):
    width = x.shape[2]
    heads = step.shape[1]
    head_dim = width // heads
    xb = x[0]
    running, steps = run[0], step[0]
    run_t = running.T
    causal = iota((BLOCK, BLOCK), 1) <= iota((BLOCK, BLOCK), 0)
    scores = jnp.where(causal, dot(c[0], b[0], ((1,), (1,))), 0.0)
    pair = 2 * head_dim
    left = iota((BLOCK, pair), 1) < head_dim
    for j in range(heads // 2):
        at = slice(j * pair, (j + 1) * pair)
        halves = []
        for h in (2 * j, 2 * j + 1):
            gap = jnp.minimum(run_t[:, h : h + 1] - running[h : h + 1], 0.0)
            mix = (scores * jnp.exp(gap) * steps[h : h + 1]).astype(BF16)
            halves.append(dot(mix, xb[:, at], ((1,), (0,))))
        inner = jnp.where(left, halves[0], halves[1])
        out[0, :, at] = inner + skip[:, at] * xb[:, at].astype(F32)


def carry_kernel(
    zx, p2, heads, core, inner, c, run, logs, own, other, came, came_log, kept, e0, *refs
):
    out, both = refs[-2:]
    width = inner.shape[2]
    head_dim = width // heads
    rows = heads * p2

    @pl.when(pl.program_id(0) == 0)
    def _():
        goes = local_index(iota((width, 1), 0), core[0], head_dim, zx, p2, heads)
        perm = (iota((width, width), 1) == goes).astype(BF16)
        enter = jnp.concatenate(
            [own[:, 0].reshape(zx * rows, -1), other[:, 0].reshape(zx * rows, -1)], axis=0
        )
        n = enter.shape[1]
        second = core[0] == 1
        past = jnp.exp(jnp.where(second, column(came_log[0, :1], rows, p2), 0.0))
        before = jnp.where(second, jnp.concatenate([came[0], kept[0]], axis=0), 0.0)
        enter = (enter.reshape(2 * zx, rows, n) * past[None]).reshape(width, n) + before
        fade = jnp.exp(column(logs[0, :1], rows, p2))
        after = (enter.reshape(2 * zx, rows, n) * fade[None]).reshape(width, n) + e0[0]
        for k, value in enumerate((enter, after)):
            both[k] = dot(perm, value.astype(BF16), ((1,), (0,))).astype(BF16)

    growth = dot(in_thirds(jnp.exp(run[0].T), 1), expander(heads, width), ((1,), (0,)))
    carry = dot(c[0], both[pl.program_id(0)], ((1,), (1,)))
    out[0] = (inner[0] + growth * carry).astype(BF16)


def merge(parts):
    top = jnp.max(parts[:, 0], axis=0)
    total = jnp.sum(parts[:, 1] * jnp.exp(parts[:, 0] - top), axis=0)
    picked = jnp.sum(parts[:, 2], axis=0)
    return top, total, picked


def full(shape):
    return pl.BlockSpec(shape, lambda *_: (0,) * len(shape))


def call(kernel, outs, *args, smem=(), anywhere=()):
    def spec(k, arg):
        if k in smem:
            return pl.BlockSpec(memory_space=pltpu.SMEM)
        if k in anywhere:
            return pl.BlockSpec(memory_space=pl.ANY)
        return full(arg.shape)

    specs = [spec(k, arg) for k, arg in enumerate(args)]
    many = isinstance(outs, tuple)
    return pl.pallas_call(
        kernel,
        grid=(1,),
        in_specs=specs,
        out_specs=tuple(full(o.shape) for o in outs) if many else full(outs.shape),
        out_shape=outs,
        compiler_params=ROOM,
    )(*args)


def shaped(*shape, dtype=F32):
    return jax.ShapeDtypeStruct(shape, dtype)


def body(
    prompt_x,
    prompt_b,
    prompt_c,
    prompt_step,
    prompt_decay,
    skip_weight,
    decode_x,
    decode_b,
    decode_c,
    decode_step,
    decode_decay,
    out_proj,
    norm_gain,
    lm_head,
    mask_words,
    state_ids,
    chosen,
):
    seqs, tokens, width = prompt_x.shape
    n = prompt_b.shape[2]
    heads = prompt_step.shape[1]
    zx, cg, grp = size_of(ZX), size_of(CG), size_of(GRP)
    p2 = decode_x.shape[3]
    rows = heads * p2
    half = width // 2
    blocks = tokens // BLOCK
    decode_rows = decode_x.shape[1]
    per = decode_rows // seqs
    many = STEPS * decode_rows
    core = lax.axis_index(CO).astype(jnp.int32)[None]

    model = out_proj.shape[2]
    wide = model // cg
    ny, nxh = lax.axis_size(Y), lax.axis_size(XH)
    iy, ixh = (lax.axis_index(a).astype(jnp.int32) for a in (Y, XH))
    grp_steps = [(dy, dx) for dy in range(ny) for dx in range(nxh)]

    def grp_perm(dy, dx):
        return [
            (y * nxh + x, (y + dy) % ny * nxh + (x + dx) % nxh)
            for y in range(ny)
            for x in range(nxh)
        ]

    w_rows = out_proj.astype(F32).reshape(rows, 2, grp, wide).transpose(1, 2, 0, 3)
    w_keep = lax.dynamic_index_in_dim(w_rows, core[0], 0, keepdims=False)
    w_other = lax.dynamic_index_in_dim(w_rows, 1 - core[0], 0, keepdims=False)
    w_came = swapped(w_other)
    w_both = jnp.stack([w_keep, w_came], axis=1)
    w_own = []
    for dy, dx in grp_steps:
        to = (iy + dy) % ny * nxh + (ixh + dx) % nxh
        part = lax.dynamic_index_in_dim(w_both, to, 0, keepdims=False)
        w_own.append(lax.ppermute(part, GRP, grp_perm(dy, dx)) if dy or dx else part)

    def by_q(value):
        shape = value.shape[2:]
        value = value.reshape(STEPS, seqs, per, *shape)
        return jnp.moveaxis(value, 1, 0).reshape(many, *shape)

    c_q, b_q = by_q(decode_c), by_q(decode_b)
    cum_q = by_q(jnp.cumsum(decode_decay, axis=0)).T
    step_q = by_q(decode_step).T
    x_q = by_q(decode_x.astype(F32).reshape(STEPS, decode_rows, rows)).T
    skip_col = jnp.repeat(skip_weight, p2)[:, None]
    vocab = lm_head.shape[1]
    first = (lax.axis_index(CTX) * size_of(GRP) + lax.axis_index(GRP)) * vocab
    chosen_q = (by_q(chosen) - first)[None]
    ids_q = by_q(state_ids)
    bits = (
        jnp.right_shift(mask_words[:, :, None], jnp.arange(32, dtype=jnp.int32)[None, None]) & 1
    ).reshape(mask_words.shape[0], vocab)
    onehot = (ids_q[None] == jnp.arange(mask_words.shape[0])[:, None]).astype(BF16)
    allowed = dot(bits.astype(BF16), onehot, ((0,), (0,)))

    by_s = lambda *shape: pl.BlockSpec((1, *shape), lambda s: (s,) + (0,) * len(shape))
    e0, keep, send, run, logs = pl.pallas_call(
        lambda *refs: states_kernel(zx, p2, *refs),
        grid=(seqs,),
        in_specs=[
            pl.BlockSpec(memory_space=pltpu.SMEM),
            by_s(tokens, width),
            by_s(tokens, n),
            by_s(heads, tokens),
            by_s(heads, tokens),
        ],
        out_specs=(
            by_s(width, n),
            by_s(half, n),
            by_s(half + 8, n),
            by_s(heads, tokens),
            by_s(8, n),
        ),
        out_shape=(
            shaped(seqs, width, n),
            shaped(seqs, half, n),
            shaped(seqs, half + 8, n),
            shaped(seqs, heads, tokens),
            shaped(seqs, 8, n),
        ),
        scratch_shapes=[pltpu.VMEM((width, width), BF16)],
        name="states",
    )(core, prompt_x, prompt_b, prompt_step, prompt_decay)
    at_k = lambda *shape: pl.BlockSpec((1, BLOCK, *shape), lambda s, k: (s, k, 0))
    lanes_k = pl.BlockSpec((1, heads, BLOCK), lambda s, k: (s, 0, k))
    came = swapped(send)
    inner = pl.pallas_call(
        inner_kernel,
        grid=(seqs, blocks),
        in_specs=[at_k(width), at_k(n), at_k(n), lanes_k, lanes_k, full((1, width))],
        out_specs=at_k(width),
        out_shape=shaped(seqs, tokens, width),
        name="inner",
    )(
        prompt_x,
        prompt_b,
        prompt_c,
        prompt_step,
        run,
        jnp.repeat(skip_weight, width // heads)[None],
    )
    pieces = pl.pallas_call(
        lambda *refs: pair_kernel(p2, heads, *refs),
        grid=(1,),
        in_specs=[
            pl.BlockSpec(memory_space=pltpu.SMEM),
            full((seqs, half, n)),
            full((seqs, 8, n)),
            full((seqs, half + 8, n)),
        ],
        out_specs=full((zx, 2 * rows + 8, n)),
        out_shape=shaped(zx, 2 * rows + 8, n),
        compiler_params=ROOM,
        name="pair",
    )(core, keep, logs, came)
    kept_other = swapped(keep)
    pieces = lax.all_to_all(pieces, ZX, 0, 0, tiled=True)
    table = shaped(rows, many)
    grow, xs, add = call(
        lambda *refs: tables_kernel(p2, heads, *refs),
        (table, table, table),
        c_q,
        b_q,
        cum_q,
        x_q,
        step_q,
        skip_col,
    )
    enter, step_y, last = call(
        lambda *refs: scan_kernel(p2, heads, *refs),
        (shaped(zx, 2 * rows, n), shaped(grp, rows, many), shaped(2 * rows, n)),
        pieces,
        c_q,
        grow,
        add,
    )
    row_state = call(rows_kernel, shaped(decode_rows, rows, n), last, b_q, grow, xs)
    decode_state = row_state.reshape(decode_rows, heads, p2, n)

    ys = lax.all_to_all(step_y, GRP, 0, 0, tiled=True)
    partial = call(
        lambda *refs: project_kernel(ny, nxh, *refs), shaped(many, wide), ys, swapped(ys), *w_own
    )
    partial = lax.all_to_all(partial.reshape(zx, many // zx, wide), ZX, 0, 0, tiled=True)
    summed = jnp.sum(partial, axis=0)
    own_cols = told(summed, ZX).reshape(many, wide)
    assert ny == 4 and nxh == 2

    def moved_y(value, by):
        return lax.ppermute(value, Y, [(i, (i + by) % ny) for i in range(ny)])

    up = moved_y(own_cols, 1)
    down = moved_y(own_cols, 3)
    across = lax.ppermute(own_cols, XH, [(0, 1), (1, 0)])
    up_2 = moved_y(up, 1)
    across_up, across_down = moved_y(across, 1), moved_y(across, 3)
    across_2 = moved_y(across_down, 3)
    blocks_y = [
        (0, 0, own_cols),
        (1, 0, up),
        (3, 0, down),
        (0, 1, across),
        (2, 0, up_2),
        (1, 1, across_up),
        (3, 1, across_down),
        (2, 1, across_2),
    ]
    steps_y = [(dy, dx) for dy, dx, _ in blocks_y]
    own_half = [value for *_, value in blocks_y]
    other_half = [swapped(value) for value in own_half]
    enter, _ = lax.optimization_barrier((enter, own_cols))

    halves = [value for pair in zip(own_half, other_half) for value in pair]
    anywhere = pl.BlockSpec(memory_space=pl.ANY)
    parts_shape = (size_of((Z, CO)), 3, many)
    parts = pl.pallas_call(
        lambda *refs: logits_kernel(ny, nxh, steps_y, *refs),
        grid=(1,),
        in_specs=[anywhere] * len(halves)
        + [full((1, model)), anywhere, full(allowed.shape), full(chosen_q.shape)],
        out_specs=full(parts_shape),
        out_shape=shaped(*parts_shape),
        scratch_shapes=[
            pltpu.VMEM((len(halves), many, wide), F32),
            pltpu.VMEM((len(halves), wide, vocab), BF16),
            pltpu.SemaphoreType.DMA((2 * len(halves),)),
        ],
        name="logits",
    )(*halves, norm_gain[None], lm_head, allowed, chosen_q)
    parts = lax.all_to_all(parts, (Z, CO), 0, 0, tiled=True)
    parts = jnp.stack(merge(parts))
    parts = told(parts, (XL, Y, XH))
    top, total, picked = merge(parts)
    logprob = picked - top - jnp.log(total)
    logprob = logprob.reshape(seqs, STEPS, per).transpose(1, 0, 2).reshape(STEPS, decode_rows)

    back = lax.all_to_all(enter, ZX, 0, 0, tiled=True).reshape(zx, seqs, rows, n)
    back_other = swapped(back)
    prompt_y = ()
    for s in range(seqs):
        of_s = lambda *shape, s=s: pl.BlockSpec((1, *shape), lambda k: (s,) + (0,) * len(shape))
        at_k = lambda *shape, s=s: pl.BlockSpec((1, BLOCK, *shape), lambda k: (s, k, 0))
        lanes_k = pl.BlockSpec((1, heads, BLOCK), lambda k, s=s: (s, 0, k))
        states_s = pl.BlockSpec((zx, 1, rows, n), lambda k, s=s: (0, s, 0, 0))
        prompt_y = pl.pallas_call(
            lambda *refs: carry_kernel(zx, p2, heads, *refs),
            grid=(blocks,),
            in_specs=[
                pl.BlockSpec(memory_space=pltpu.SMEM),
                at_k(width),
                at_k(n),
                lanes_k,
                of_s(8, n),
                states_s,
                states_s,
                of_s(half, n),
                pl.BlockSpec((1, 8, n), lambda k, s=s: (s, half // 8, 0)),
                of_s(half, n),
                of_s(width, n),
                *[pl.BlockSpec(memory_space=pl.ANY) for _ in prompt_y],
            ],
            out_specs=at_k(width),
            out_shape=shaped(seqs, tokens, width, dtype=BF16),
            input_output_aliases={11: 0} if prompt_y else {},
            scratch_shapes=[pltpu.VMEM((blocks, width, n), BF16)],
        )(core, inner, prompt_c, run, logs, back, back_other, came, came, kept_other, e0, *prompt_y)
        prompt_y = (prompt_y,)
    (prompt_y,) = prompt_y
    return (prompt_y, decode_state, logprob)


def solution(mesh):
    ctx, grp = mesh.devices.shape
    shape = (ctx // 4, 2, 2, grp // 2, 2)
    finer = Mesh(mesh.devices.reshape(shape), ALL)
    in_specs = (
        P(None, CTX, GRP),
        P(None, CTX, GRP),
        P(None, CTX, GRP),
        P(None, GRP, CTX),
        P(None, GRP, CTX),
        P(GRP),
        P(None, None, GRP, CTX),
        P(None, None, GRP),
        P(None, None, GRP),
        P(None, None, GRP),
        P(None, None, GRP),
        P(GRP, CTX, None),
        P(),
        P(None, ALL),
        P(None, ALL),
        P(),
        P(),
    )
    out_specs = (P(None, CTX, GRP), P(None, GRP, CTX, None), P())

    return jax.shard_map(body, mesh=finer, in_specs=in_specs, out_specs=out_specs, check_vma=False)
```
